32 devices in a mesh: groups: 2 (over x), seq: 16 (over z, y, core).
Axes of the slice: x: 2, y: 2, z: 4, core: 2. Of those that a mesh axis runs over, the one named last changes fastest.
Arguments:
- mixed_qkv: bfloat16 [4096, 8192], P(('groups', 'seq')), parts along dimension 0, may hold values from -6 to 6
- conv_weight: bfloat16 [4, 8192], replicated, may hold values from -3 to 3
- beta_logit: bfloat16 [4096, 32], P(('groups', 'seq')), parts along dimension 0
- log_decay: float32 [4096, 32], P(('groups', 'seq')), parts along dimension 0
- gate_in: bfloat16 [4096, 4096], P(('groups', 'seq')), parts along dimension 0, may hold values from -6 to 6
- norm_gain: float32 [128], replicated, may hold values from 0.1 to 1.9
Outputs:
- layer_out: bfloat16 [4096, 4096], P(('groups', 'seq')), parts along dimension 0
The draws below stay inside these ranges and needn't reach their ends.
There are 2 independent parts, one for each index of `groups`. The reference program is written for one: setup_inputs(seed, part) draws one part's arguments, and reference() takes and returns one part's arrays. A program takes and returns all parts, laid end to end along the dimension named above; an argument that names none is the same for every part. Nothing has to cross between parts.
All inputs are finite; a program needn't handle non-finite values.
Results may differ from the reference program's by a relative error of at most 0.0044.
Values may be sent and summed in bfloat16 or wider, within the bound.
No kernel may reach another device: no remote copies, remote signals or barrier semaphores. Data moves between devices by JAX's collectives and lax.ppermute only.
A program may use at most 128 MiB of HBM per device.

```python
import math
import jax
import jax.numpy as jnp
from jax import lax

KH = 16
VH = 32
DH = 128
KW = 4
CH = 128
TOK_DEV = 128
DOCUMENT_TOKENS = 2048
CONV = 8192


def slow_heads_of(key):
    shuffled = jax.random.permutation(jax.random.fold_in(key, 11), VH)
    slow_count = VH // 2
    return shuffled < slow_count


def rough_factor(key, shape):
    return jnp.clip(1.05 + 0.2 * jax.random.normal(key, shape, jnp.float32), 0.7, 1.4)


def draw_log_decay(key, part):
    slow_heads = slow_heads_of(key)
    token_positions = jnp.arange(DOCUMENT_TOKENS)
    fast_rate = jnp.exp(jax.random.uniform(jax.random.fold_in(key, 1), (VH,), jnp.float32, math.log(1.0 / 50.0), math.log(1.0 / 30.0)))
    slow_rate = jnp.exp(jax.random.uniform(jax.random.fold_in(key, 2), (VH,), jnp.float32, math.log(0.05), math.log(0.2))) / DOCUMENT_TOKENS
    base_rate = jnp.where(slow_heads, slow_rate, fast_rate)
    block_factor = jnp.exp(jax.random.uniform(jax.random.fold_in(key, 3), (DOCUMENT_TOKENS // TOK_DEV, VH), jnp.float32, math.log(0.5), math.log(2.0)))
    token_frequency = base_rate[None, :] * block_factor[token_positions // TOK_DEV] * rough_factor(jax.random.fold_in(key, 4), (DOCUMENT_TOKENS, VH))
    surge_position = jax.random.randint(jax.random.fold_in(key, 5), (3,), 0, DOCUMENT_TOKENS)
    surge_count = jax.random.randint(jax.random.fold_in(key, 6), (), 1, 4)
    active_flag = jnp.arange(3) < surge_count
    retain_fraction = jax.random.uniform(jax.random.fold_in(key, 7), (3, VH), jnp.float32, 0.65, 0.8)
    surge_mask = (token_positions[:, None] == surge_position[None, :]) & active_flag[None, :]
    surge_logarithm = jnp.sum(jnp.where(surge_mask[:, :, None], jnp.log(retain_fraction)[None, :, :], 0.0), axis=1)
    return jnp.where(jnp.any(surge_mask, axis=1)[:, None], surge_logarithm, -token_frequency).astype(jnp.float32)


def draw_beta_logit(key, part):
    slow_heads = slow_heads_of(key)
    erase_share = jnp.exp(jax.random.uniform(jax.random.fold_in(key, 8), (VH,), jnp.float32, math.log(0.1), math.log(0.3)))
    slow_beta = erase_share[None, :] * DH / DOCUMENT_TOKENS * rough_factor(jax.random.fold_in(key, 9), (DOCUMENT_TOKENS, VH))
    slow_logit = jnp.log(slow_beta) - jnp.log1p(-slow_beta)
    fast_logit = jnp.clip(jax.random.normal(jax.random.fold_in(key, 10), (DOCUMENT_TOKENS, VH), jnp.float32), -3.0, 3.0)
    return jnp.where(slow_heads[None, :], slow_logit, fast_logit).astype(jnp.bfloat16)


def levels(own_key, dims, cuts, smallest, top_value):
    gain, own = 1.0, jax.random.fold_in(own_key, 6)
    for axis_at, shards_of in cuts:
        heights = jnp.exp(jax.random.uniform(jax.random.fold_in(own, axis_at), (shards_of,), jnp.float32, smallest / len(cuts), top_value / len(cuts)))
        gain = gain * jnp.repeat(heights, dims[axis_at] // shards_of).reshape([-1 if axis == axis_at else 1 for axis in range(len(dims))])
    return gain


def scatter_about(rng, shape, width, most, cuts=(), held_as=jnp.bfloat16):
    entries = width * jax.random.normal(rng, shape, jnp.float32)
    if cuts:
        entries = entries * levels(rng, shape, cuts, -0.22, 0.18)
    return jnp.clip(entries, -most, most).astype(held_as)


def setup_inputs(seed: int = 0, part: int = 0) -> dict:
    seeds = jax.random.split(jax.random.key(seed), 7)
    part_keys = jax.random.split(jax.random.fold_in(seeds[6], part), 7)
    mixed_qkv = scatter_about(part_keys[0], (DOCUMENT_TOKENS, CONV), 1.0, 6.0, ((0, 16),))
    conv_weight = scatter_about(seeds[1], (KW, CONV), KW ** -0.5, 3.0)
    beta_logit = draw_beta_logit(jax.random.fold_in(jax.random.fold_in(seeds[6], part), 71), part)
    log_decay = draw_log_decay(jax.random.fold_in(jax.random.fold_in(seeds[6], part), 71), part)
    gate_in = scatter_about(part_keys[4], (DOCUMENT_TOKENS, VH * DH), 1.0, 6.0, ((0, 16),))
    norm_gain = jnp.clip(1.0 + 0.18 * jax.random.normal(seeds[5], (DH,), jnp.float32), 0.1, 1.9)
    return dict(mixed_qkv=mixed_qkv, conv_weight=conv_weight, beta_logit=beta_logit, log_decay=log_decay, gate_in=gate_in, norm_gain=norm_gain)


HIGHEST = lax.Precision.HIGHEST

def unit_rows(values):
    return values * lax.rsqrt(lax.optimization_barrier(jnp.sum(values * values, axis=-1, keepdims=True)) + 1e-06)

def convolve(padded, conv_weight, row_count):
    tap_count = conv_weight.shape[0]
    conv_sum = jnp.zeros((row_count, padded.shape[1]), jnp.float32)
    for tap_index in range(tap_count):
        conv_sum = conv_sum + padded[tap_index:tap_index + row_count].astype(jnp.float32) * conv_weight[tap_index].astype(jnp.float32)
    return jax.nn.silu(conv_sum).astype(jnp.bfloat16)

def split_heads(conv_out):
    row_count = conv_out.shape[0]
    key_cols = KH * DH
    query_rows = unit_rows(conv_out[:, :key_cols].astype(jnp.float32).reshape(row_count, KH, DH)) * DH ** (-0.5)
    key_rows = unit_rows(conv_out[:, key_cols:2 * key_cols].astype(jnp.float32).reshape(row_count, KH, DH))
    value_rows = conv_out[:, 2 * key_cols:].astype(jnp.float32).reshape(row_count, VH, DH)
    return (query_rows, key_rows, value_rows)

def span_terms(query_rows, key_rows, value_rows, beta_rows, decay_log):
    block_len = query_rows.shape[0]
    head_width = query_rows.shape[2]
    head_repeat = value_rows.shape[1] // key_rows.shape[1]
    lower_mask = jnp.tril(jnp.ones((block_len, block_len), jnp.float32))
    identity_block = jnp.eye(block_len, dtype=jnp.float32)
    strict_mask = lower_mask - identity_block
    cumulative = jnp.dot(lower_mask, decay_log, precision=HIGHEST).T
    log_gaps = cumulative[:, :, None] - cumulative[:, None, :]
    decay_pair = jnp.exp(jnp.minimum(log_gaps, 0.0)) * lower_mask
    key_dot = jnp.repeat(jnp.einsum('tgd,sgd->gts', key_rows, key_rows, precision=HIGHEST), head_repeat, axis=0)
    query_dot = jnp.repeat(jnp.einsum('tgd,sgd->gts', query_rows, key_rows, precision=HIGHEST), head_repeat, axis=0)
    keys_head = jnp.repeat(key_rows, head_repeat, axis=1).transpose(1, 0, 2)
    query_head = jnp.repeat(query_rows, head_repeat, axis=1).transpose(1, 0, 2)
    values_head = value_rows.transpose(1, 0, 2)
    beta_head = beta_rows.T
    growth = jnp.exp(cumulative)
    system = identity_block + beta_head[:, :, None] * decay_pair * key_dot * strict_mask
    right_side = jnp.concatenate([(beta_head * growth)[:, :, None] * keys_head, beta_head[:, :, None] * values_head], axis=2)
    solved = jax.scipy.linalg.solve_triangular(system, right_side, lower=True, unit_diagonal=True)
    w_rows = solved[:, :, :head_width]
    u_rows = solved[:, :, head_width:]
    mixing = decay_pair * query_dot
    local_out = jnp.einsum('hts,hsd->htd', mixing, u_rows, precision=HIGHEST)
    carry_map = growth[:, :, None] * query_head - jnp.einsum('hts,hsk->htk', mixing, w_rows, precision=HIGHEST)
    key_tail = jnp.exp(cumulative[:, -1:] - cumulative)[:, :, None] * keys_head
    transition = growth[:, -1][:, None, None] * jnp.eye(head_width, dtype=jnp.float32) - jnp.einsum('hsk,hsj->hkj', w_rows, key_tail, precision=HIGHEST)
    state_add = jnp.einsum('hsv,hsk->hvk', u_rows, key_tail, precision=HIGHEST)
    return (carry_map, local_out, transition, state_add)

def gated_norm(core_out, gate_in, norm_gain):
    mean_sq = lax.optimization_barrier(jnp.mean(core_out * core_out, axis=-1, keepdims=True))
    gate_val = gate_in.astype(jnp.float32).reshape(core_out.shape)
    scaled = core_out * lax.rsqrt(mean_sq + 1e-06) * norm_gain * jax.nn.silu(gate_val)
    return scaled.astype(jnp.bfloat16).reshape(core_out.shape[0], core_out.shape[1] * core_out.shape[2])

def reference(mixed_qkv, conv_weight, beta_logit, log_decay, gate_in, norm_gain):
    span_count = DOCUMENT_TOKENS // CH

    def advance(carried, pieces):
        state_now, prior_rows = carried
        raw_rows, beta_part, decay_part, gate_part = pieces
        padded = jnp.concatenate([prior_rows, raw_rows], axis=0)
        conv_out = convolve(padded, conv_weight, CH)
        query_rows, key_rows, value_rows = split_heads(conv_out)
        beta_rows = jax.nn.sigmoid(beta_part.astype(jnp.float32))
        carry_map, local_out, transition, state_add = span_terms(query_rows, key_rows, value_rows, beta_rows, decay_part)
        core_out = local_out + jnp.einsum('htk,hvk->htv', carry_map, state_now, precision=HIGHEST)
        new_state = jnp.einsum('hvk,hkj->hvj', state_now, transition, precision=HIGHEST) + state_add
        out_rows = gated_norm(core_out.transpose(1, 0, 2), gate_part, norm_gain)
        return ((new_state, padded[CH:]), out_rows)
    start_carry = (jnp.zeros((VH, DH, DH), jnp.float32), jnp.zeros((KW - 1, CONV), jnp.bfloat16))
    pieces = (mixed_qkv.reshape(span_count, CH, CONV), beta_logit.reshape(span_count, CH, VH), log_decay.reshape(span_count, CH, VH), gate_in.reshape(span_count, CH, VH * DH))
    _, outputs = lax.scan(advance, start_carry, pieces)
    return outputs.reshape(DOCUMENT_TOKENS, VH * DH)
```

```python
import functools

import jax
import jax.numpy as jnp
from jax import lax
from jax.experimental import pallas as pl
from jax.experimental.pallas import tpu as pltpu
from jax.sharding import PartitionSpec as P

KH = 16
VH = 32
DH = 128
CH = 128
CHIPS = 4
PIECE = 4
ROWS = PIECE * DH + 16
WIDE = 2 * DH

F32 = jnp.float32
BF16 = jnp.bfloat16


def dot(a, b):
    return jnp.dot(a, b, preferred_element_type=F32)


def halves(x):
    high = x.astype(BF16)
    return high, (x - high.astype(F32)).astype(BF16)


def decay_rows(decays):
    high, low = halves(decays)
    return jnp.concatenate([high, low], axis=0)


def decays_of(rows):
    rows = rows.astype(F32)
    return rows[:8] + rows[8:]


def head_slice(h):
    return slice(h * DH, (h + 1) * DH)


def terms_kernel(
    sc_ref, xq, xk, xv, pq, pk, pv, wq, wk, wv, rows_ref, masks_ref, ma_ref, loc_ref, car_ref, scr
):
    convs = []
    at = 0
    for x_ref, p_ref, w_ref in ((xq, pq, wq), (xk, pk, wk), (xv, pv, wv)):
        width = x_ref.shape[1]
        cols = slice(at, at + width)
        scr[0:8, cols] = p_ref[...].astype(F32)
        scr[8 : 8 + CH, cols] = x_ref[...].astype(F32)
        w = w_ref[...].astype(F32)
        total = scr[5 : 5 + CH, cols] * w[0:1]
        for tap in range(1, 4):
            total = total + scr[5 + tap : 5 + tap + CH, cols] * w[tap : tap + 1]
        convs.append((total / (1.0 + jnp.exp(-total))).astype(BF16))
        at += width
    cq, ck, cv = convs

    rows = rows_ref[0]
    cols = rows.T
    grow_cols = jnp.exp(cols)
    tail_rows = jnp.exp(rows[:, CH - 1 : CH] - rows)
    ma_ref[0, PIECE * DH :, :] = decay_rows(
        jnp.broadcast_to(jnp.exp(rows[:, CH - 1 : CH]), (8, WIDE))
    )

    t_at = lax.broadcasted_iota(jnp.int32, (CH, CH), 0)
    s_at = lax.broadcasted_iota(jnp.int32, (CH, CH), 1)
    lower = t_at >= s_at
    strict = t_at > s_at
    unit = (t_at == s_at).astype(F32)

    per_head = []
    for g in range(PIECE // 2):
        q_b, k_b = cq[:, head_slice(g)], ck[:, head_slice(g)]
        q_f, k_f = q_b.astype(F32), k_b.astype(F32)
        k_t = k_f.T
        rq_col = lax.rsqrt(jnp.sum(q_f * q_f, axis=1, keepdims=True) + 1e-06) * DH ** (-0.5)
        rk_col = lax.rsqrt(jnp.sum(k_f * k_f, axis=1, keepdims=True) + 1e-06)
        rk_row = lax.rsqrt(jnp.sum(k_t * k_t, axis=0, keepdims=True) + 1e-06)
        gram = dot(jnp.concatenate([q_b, k_b], axis=0), k_t.astype(BF16))
        query_dot = gram[:CH] * rq_col * rk_row
        key_dot = gram[CH:] * rk_col * rk_row
        for i in range(2):
            h = 2 * g + i
            pair = jnp.where(lower, jnp.exp(jnp.minimum(cols[:, h : h + 1] - rows[h : h + 1], 0.0)), 0.0)
            system = jnp.where(strict, key_dot * pair * cols[:, 4 + h : 5 + h], 0.0)
            per_head.append(
                dict(
                    h=h,
                    mixing=halves(query_dot * pair),
                    system=system.astype(BF16),
                    key_gain=(k_f * (grow_cols[:, h : h + 1] * rk_col)).astype(BF16),
                    query=q_f * (grow_cols[:, h : h + 1] * rq_col),
                    tail=halves(k_t * (rk_row * tail_rows[h : h + 1])),
                )
            )
            first = unit - system * masks_ref[0].astype(F32)
            per_head[-1]["inv"] = halves(first)

    for level in range(1, 7):
        mask = masks_ref[level]
        steps = [dot(p["inv"][0], p["system"] * mask) for p in per_head]
        steps = [dot(s.astype(BF16), p["inv"][0]) for s, p in zip(steps, per_head)]
        for s, p in zip(steps, per_head):
            high, low = halves(s)
            p["inv"] = (p["inv"][0] - high, p["inv"][1] - low)

    for p in per_head:
        h = p["h"]
        inv = halves((p["inv"][0].astype(F32) + p["inv"][1].astype(F32)) * rows[4 + h : 5 + h])
        right = jnp.concatenate([p["key_gain"], cv[:, head_slice(h)]], axis=1)
        p["solved"] = dot(
            jnp.concatenate(inv, axis=1), jnp.concatenate([right, right], axis=0)
        ).astype(BF16)
    for p in per_head:
        h = p["h"]
        left = jnp.concatenate(
            [jnp.concatenate(p["mixing"], axis=1), jnp.concatenate(p["tail"], axis=1)], axis=0
        )
        both = dot(left, jnp.concatenate([p["solved"], p["solved"]], axis=0))
        ma_ref[0, head_slice(h), :] = both[CH:].astype(BF16)
        loc_ref[0, h] = both[:CH, DH:]
        car_ref[0, h] = jnp.concatenate(halves(p["query"] - both[:CH, :DH]), axis=1)


def block_terms(owner, mixed_qkv, rim, conv_weight, rows, masks):
    pieces = VH // 2 // PIECE
    kd, vd = PIECE // 2 * DH, PIECE * DH
    key_blocks = KH * DH // kd

    def at(first):
        return lambda i, sc: (0, first + pieces * sc[0] + i)

    specs = []
    for height in (CH, 8, conv_weight.shape[0]):
        specs += [
            pl.BlockSpec((height, kd), at(0)),
            pl.BlockSpec((height, kd), at(key_blocks)),
            pl.BlockSpec((height, vd), at(2 * KH * DH // vd)),
        ]
    out_specs = [
        pl.BlockSpec((1, ROWS, WIDE), lambda i, sc: (i, 0, 0)),
        pl.BlockSpec((1, PIECE, CH, DH), lambda i, sc: (i, 0, 0, 0)),
        pl.BlockSpec((1, PIECE, CH, WIDE), lambda i, sc: (i, 0, 0, 0)),
    ]
    return pl.pallas_call(
        terms_kernel,
        out_shape=[
            jax.ShapeDtypeStruct((pieces, ROWS, WIDE), BF16),
            jax.ShapeDtypeStruct((pieces, PIECE, CH, DH), F32),
            jax.ShapeDtypeStruct((pieces, PIECE, CH, WIDE), BF16),
        ],
        grid_spec=pltpu.PrefetchScalarGridSpec(
            num_scalar_prefetch=1,
            grid=(pieces,),
            in_specs=specs
            + [
                pl.BlockSpec((1, 8, CH), lambda i, sc: (pieces * sc[0] + i, 0, 0)),
                pl.BlockSpec((7, CH, CH), lambda i, sc: (0, 0, 0)),
            ],
            out_specs=out_specs,
            scratch_shapes=[pltpu.VMEM((CH + 8, 2 * kd + vd), F32)],
        ),
        cost_estimate=pl.CostEstimate(flops=2_000_000_000, bytes_accessed=6_000_000, transcendentals=0),
        name="block_terms",
    )(
        owner,
        *([mixed_qkv] * 3),
        *([rim] * 3),
        *([conv_weight] * 3),
        rows,
        masks,
    )


def compose_kernel(sc_ref, mine_ref, theirs_ref, out_ref):
    is_first = sc_ref[0] == 0
    mine_g, theirs_g = decays_of(mine_ref[0, PIECE * DH :]), decays_of(theirs_ref[0, PIECE * DH :])
    first_g = jnp.where(is_first, mine_g, theirs_g)
    second_g = jnp.where(is_first, theirs_g, mine_g)
    for h in range(PIECE):
        mine, theirs = mine_ref[0, head_slice(h)], theirs_ref[0, head_slice(h)]
        first = jnp.where(is_first, mine, theirs)
        second = jnp.where(is_first, theirs, mine)
        product = dot(second[:, :DH], first)
        kept = jnp.concatenate(
            [second[:, :DH].astype(F32) * first_g[h : h + 1, :DH], second[:, DH:].astype(F32)],
            axis=1,
        )
        joined = first.astype(F32) * second_g[h : h + 1] - product + kept
        out_ref[head_slice(h), :] = joined.astype(BF16)
    out_ref[PIECE * DH :, :] = decay_rows(first_g * second_g)


def compose(place, mine, theirs, offset):
    spec = pl.BlockSpec((1, ROWS, WIDE), lambda i, sc: (sc[1] ^ offset, 0, 0))
    return pl.pallas_call(
        compose_kernel,
        out_shape=jax.ShapeDtypeStruct((ROWS, WIDE), BF16),
        grid_spec=pltpu.PrefetchScalarGridSpec(
            num_scalar_prefetch=1,
            grid=(1,),
            in_specs=[spec, spec],
            out_specs=pl.BlockSpec((ROWS, WIDE), lambda i, sc: (0, 0)),
        ),
        cost_estimate=pl.CostEstimate(flops=40_000_000, bytes_accessed=900_000, transcendentals=0),
        name="compose",
    )(place, mine, theirs)


def advance(ref, slot, h, state):
    decays = decays_of(ref[slot, PIECE * DH :])
    mats = ref[slot, head_slice(h)]
    return (
        state.astype(F32) * decays[h : h + 1, :DH]
        - dot(mats[:, :DH], state)
        + mats[:, DH:].astype(F32)
    )


def gather_kernel(sc_ref, p0, p1, p2, p3, in_ref, order_ref, out_ref):
    for offset, piece in enumerate((p0, p1, p2, p3)):
        order_ref[sc_ref[1] ^ offset] = piece[...]
    for h in range(PIECE):
        state = in_ref[h]
        for chip in range(CHIPS):
            state = advance(order_ref, chip, h, state).astype(BF16)
        out_ref[h] = state


def spread_kernel(sc_ref, order_ref, in_ref, o0, o1, o2, o3, scr):
    for h in range(PIECE):
        state = in_ref[h]
        for chip in range(CHIPS):
            scr[chip, h] = state
            if chip < CHIPS - 1:
                state = advance(order_ref, chip, h, state).astype(BF16)
    for offset, out in enumerate((o0, o1, o2, o3)):
        out[...] = scr[sc_ref[1] ^ offset]


def scalar_call(kernel, place, args, out_shape, scratch=(), name=None):
    vmem = pl.BlockSpec(memory_space=pltpu.VMEM)
    return pl.pallas_call(
        kernel,
        out_shape=out_shape,
        in_specs=[pl.BlockSpec(memory_space=pltpu.SMEM)] + [vmem] * len(args),
        out_specs=jax.tree.map(lambda _: vmem, out_shape),
        scratch_shapes=list(scratch),
        cost_estimate=pl.CostEstimate(flops=100_000_000, bytes_accessed=2_000_000, transcendentals=0),
        name=name,
    )(place, *args)


def enter_kernel(sc_ref, mine_ref, theirs_ref, p0, p1, p2, p3, keep_ref, send_ref, scr):
    for offset, piece in enumerate((p0, p1, p2, p3)):
        scr[sc_ref[1] ^ offset] = piece[...]

    def finish(first_ref, start_ref, next_ref):
        for i in range(CHIPS):
            for h in range(PIECE):
                start = scr[i, h]
                start_ref[i, h] = start
                next_ref[i, h] = advance(first_ref, i, h, start).astype(BF16)

    @pl.when(sc_ref[0] == 0)
    def _():
        finish(mine_ref, keep_ref, send_ref)

    @pl.when(sc_ref[0] == 1)
    def _():
        finish(theirs_ref, send_ref, keep_ref)


def finish_kernel(sc_ref, loc_ref, car_ref, state_ref, gate_ref, gain_ref, *refs):
    out_ref = refs[-1]
    for h in range(PIECE):
        state = state_ref[0, h]
        core = loc_ref[0, h] + dot(car_ref[0, h], jnp.concatenate([state, state], axis=0))
        mean_sq = jnp.mean(core * core, axis=1, keepdims=True)
        gate = gate_ref[:, head_slice(h)].astype(F32)
        scaled = core * lax.rsqrt(mean_sq + 1e-06) * gain_ref[...] * (gate / (1.0 + jnp.exp(-gate)))
        out_ref[:, head_slice(h)] = scaled.astype(BF16)


def finish(owner, local_out, carry_map, state, gate_in, gain, so_far):
    pieces = VH // 2 // PIECE
    cols = pl.BlockSpec((CH, PIECE * DH), lambda i, sc: (0, pieces * sc[0] + i))
    in_specs = [
        pl.BlockSpec((1, PIECE, CH, DH), lambda i, sc: (i, 0, 0, 0)),
        pl.BlockSpec((1, PIECE, CH, WIDE), lambda i, sc: (i, 0, 0, 0)),
        pl.BlockSpec((1, PIECE, DH, DH), lambda i, sc: (i, 0, 0, 0)),
        cols,
        pl.BlockSpec((1, DH), lambda i, sc: (0, 0)),
    ]
    args = [owner, local_out, carry_map, state, gate_in, gain]
    aliases = {}
    if so_far is not None:
        in_specs.append(pl.BlockSpec(memory_space=pl.ANY))
        aliases = {len(args): 0}
        args.append(so_far)
    return pl.pallas_call(
        finish_kernel,
        out_shape=jax.ShapeDtypeStruct(gate_in.shape, BF16),
        grid_spec=pltpu.PrefetchScalarGridSpec(
            num_scalar_prefetch=1, grid=(pieces,), in_specs=in_specs, out_specs=cols
        ),
        input_output_aliases=aliases,
        cost_estimate=pl.CostEstimate(flops=300_000_000, bytes_accessed=4_000_000, transcendentals=0),
        name="finish",
    )(*args)


def shift(block, distance):
    count = lax.axis_size("seq")
    return lax.ppermute(block, "seq", [(i, i + distance) for i in range(count - distance)])


def swap(block, distance):
    return lax.ppermute(block, "seq", [(i, i ^ distance) for i in range(lax.axis_size("seq"))])


def level_masks():
    t_at = lax.broadcasted_iota(jnp.int32, (7, CH, CH), 1)
    s_at = lax.broadcasted_iota(jnp.int32, (7, CH, CH), 2)
    level = lax.broadcasted_iota(jnp.int32, (7, CH, CH), 0)
    return ((t_at > s_at) & ((t_at ^ s_at) >> level == 1)).astype(BF16)


def local(mixed_qkv, conv_weight, beta_logit, log_decay, gate_in, norm_gain):
    at = lax.axis_index("seq")
    core, chip = at % 2, (at // 2) % CHIPS
    rim = shift(mixed_qkv[CH - 8 :], 1)
    mine_at, theirs_at = core[None], (1 - core)[None]
    place = jnp.stack([core, chip])

    upper = jnp.triu(jnp.ones((CH, CH), F32))
    cumulative = jnp.einsum("sh,st->ht", log_decay, upper, precision=lax.Precision.HIGHEST)
    beta = jax.nn.sigmoid(beta_logit.astype(F32)).T
    rows = jnp.concatenate(
        [cumulative.reshape(-1, PIECE, CH), beta.reshape(-1, PIECE, CH)], axis=1
    )
    masks = level_masks()

    theirs_ma, theirs_loc, theirs_car = block_terms(
        theirs_at, mixed_qkv, rim, conv_weight, rows, masks
    )
    other_ma = swap(theirs_ma, 1)
    mine_ma, mine_loc, mine_car = block_terms(mine_at, mixed_qkv, rim, conv_weight, rows, masks)

    sent = [compose(place, mine_ma, other_ma, offset) for offset in range(CHIPS)]
    pieces = [sent[0]] + [swap(sent[offset], 2 * offset) for offset in range(1, CHIPS)]

    state_shape = jax.ShapeDtypeStruct((PIECE, DH, DH), BF16)
    order_shape = jax.ShapeDtypeStruct((CHIPS, ROWS, WIDE), BF16)
    entering = jnp.zeros((PIECE, DH, DH), BF16)
    for _ in range(lax.axis_size("seq") // (2 * CHIPS) - 1):
        order, leaving = scalar_call(
            gather_kernel, place, [*pieces, entering], [order_shape, state_shape], name="gather"
        )
        entering = shift(leaving, 2 * CHIPS)
    spread = scalar_call(
        spread_kernel,
        place,
        [order, entering],
        [state_shape] * CHIPS,
        [pltpu.VMEM((CHIPS, PIECE, DH, DH), BF16)],
        name="spread",
    )
    starts = [spread[0]] + [swap(spread[offset], 2 * offset) for offset in range(1, CHIPS)]
    states_shape = jax.ShapeDtypeStruct((CHIPS, PIECE, DH, DH), BF16)
    keep, send = scalar_call(
        enter_kernel,
        place,
        [mine_ma, other_ma, *starts],
        [states_shape, states_shape],
        [pltpu.VMEM((CHIPS, PIECE, DH, DH), BF16)],
        name="enter",
    )
    given = swap(send, 1)
    gain = norm_gain[None]
    out = finish(mine_at, mine_loc, mine_car, keep, gate_in, gain, None)
    return finish(theirs_at, theirs_loc, theirs_car, given, gate_in, gain, out)


def solution(mesh):
    spec = P(("groups", "seq"), None)
    return jax.shard_map(
        local,
        mesh=mesh,
        in_specs=(spec, P(), spec, spec, spec, P()),
        out_specs=spec,
        check_vma=False,
    )
```

```python
import functools

import jax
import jax.numpy as jnp
import ml_dtypes
import numpy as np
from jax import lax
from jax.experimental import pallas as pl
from jax.experimental.pallas import tpu as pltpu
from jax.sharding import PartitionSpec as P

KH = 16
VH = 32
DH = 128
CH = 128
CHIPS = 4
PIECE = 4
BANDS = ((0, 1),)
WIDE = 2 * DH

F32 = jnp.float32
BF16 = jnp.bfloat16


def dot(a, b):
    return jnp.dot(a, b, preferred_element_type=F32)


def halves(x):
    high = x.astype(BF16)
    return high, (x - high.astype(F32)).astype(BF16)


def decay_rows(decays):
    high, low = halves(decays)
    return jnp.concatenate([high, low], axis=0)


def rows_of(keys):
    return 2 * len(keys) * DH + 16


def decays_of(rows):
    rows = rows.astype(F32)
    return rows[:8] + rows[8:]


def head_slice(h):
    return slice(h * DH, (h + 1) * DH)


def rows_kernel(decay_ref, logit_ref, rows_ref):
    s_at = lax.broadcasted_iota(jnp.int32, (CH, CH), 0)
    t_at = lax.broadcasted_iota(jnp.int32, (CH, CH), 1)
    cumulative = jnp.dot(
        decay_ref[...],
        (s_at <= t_at).astype(F32),
        precision=lax.Precision.HIGHEST,
        preferred_element_type=F32,
    )
    beta = 1.0 / (1.0 + jnp.exp(-logit_ref[...].astype(F32)))
    for g in range(VH // PIECE):
        rows_ref[g, :PIECE] = cumulative[g * PIECE : (g + 1) * PIECE]
        rows_ref[g, PIECE:] = beta[g * PIECE : (g + 1) * PIECE]


def taps(padded, w, height):
    total = padded(0) * w[0:1]
    for tap in range(1, 4):
        total = total + padded(tap) * w[tap : tap + 1]
    return (total / (1.0 + jnp.exp(-total))).astype(BF16)


def conv_kernel(sc_ref, x_ref, w_ref, out_ref, scr):
    scr[...] = x_ref[...].astype(F32)
    w = w_ref[...].astype(F32)
    out_ref[8:] = taps(lambda tap: scr[5 + tap : 5 + tap + CH - 8, :], w, CH - 8)


def early_conv(place, mixed_qkv, conv_weight):
    width = 512
    keys, values = KH // 2 * DH // width, VH // 2 * DH // width

    def at(i, sc):
        owner = 1 - sc[0]
        key_at = KH * DH // width + owner * keys + i
        value_at = 2 * KH * DH // width + owner * values + i - keys
        return (0, jnp.where(i < keys, key_at, value_at))

    tall = pl.BlockSpec((CH, width), at)
    return pl.pallas_call(
        conv_kernel,
        out_shape=jax.ShapeDtypeStruct(mixed_qkv.shape, BF16),
        grid_spec=pltpu.PrefetchScalarGridSpec(
            num_scalar_prefetch=1,
            grid=(keys + values,),
            in_specs=[tall, pl.BlockSpec((conv_weight.shape[0], width), at)],
            out_specs=tall,
            scratch_shapes=[pltpu.VMEM((CH, width), F32)],
        ),
        cost_estimate=pl.CostEstimate(flops=10_000_000, bytes_accessed=2_000_000, transcendentals=0),
        compiler_params=pltpu.CompilerParams(vmem_limit_bytes=8 << 20),
        name="conv",
    )(place, mixed_qkv, conv_weight)


def convolved(x_ref, rim_ref, w_ref, scr, slot, column, width, conv_ref=None):
    cols = pl.ds(pl.multiple_of(column, DH), width)
    w = w_ref[:, cols].astype(F32)
    scr[slot, 0:8, :width] = rim_ref[:, cols].astype(F32)
    if conv_ref is None:
        scr[slot, 8 : 8 + CH, :width] = x_ref[:, cols].astype(F32)
        return taps(lambda tap: scr[slot, 5 + tap : 5 + tap + CH, :width], w, CH).astype(F32)
    scr[slot, 8:16, :width] = x_ref[:8, cols].astype(F32)
    first = taps(lambda tap: scr[slot, 5 + tap : 13 + tap, :width], w, 8)
    rest = conv_ref[:, cols].astype(F32)
    return jnp.concatenate([first.astype(F32), rest[8:]], axis=0)


def inverse_norms(rows, axis):
    return lax.rsqrt(jnp.sum(rows * rows, axis=axis, keepdims=True) + 1e-06)


def decay_pairs(rows, cols, h, lower):
    gap = jnp.minimum(cols[:, h : h + 1] - rows[h : h + 1], 0.0)
    return jnp.where(lower, jnp.exp(gap), 0.0)


def token_order():
    t_at = lax.broadcasted_iota(jnp.int32, (CH, CH), 0)
    s_at = lax.broadcasted_iota(jnp.int32, (CH, CH), 1)
    return t_at, s_at


def terms_kernel(keys, sc_ref, x_ref, rim_ref, w_ref, conv_ref, rows_ref, masks_ref, *refs):
    theirs_refs, mine_refs, scr = refs[:3], refs[3:6], refs[6]
    t_at, s_at = token_order()
    lower, strict = t_at >= s_at, t_at > s_at
    unit = (t_at == s_at).astype(F32)
    pieces = VH // 2 // PIECE
    kd, vd = len(keys) * DH, 2 * len(keys) * DH

    heads = []
    slot = 0
    for own, (ma_ref, solved_ref, key_ref) in enumerate((theirs_refs, mine_refs)):
        owner = sc_ref[0] if own else 1 - sc_ref[0]
        conv = functools.partial(
            convolved, x_ref, rim_ref, w_ref, scr, conv_ref=None if own else conv_ref
        )
        for offset in range(CHIPS):
            piece = owner * pieces + (sc_ref[1] ^ offset)
            key_at = piece * PIECE // 2 + keys[0]
            ck = conv(slot, (KH + key_at) * DH, kd)
            cv = conv(slot + 1, 2 * (KH + key_at) * DH, vd)
            slot += 2
            rows = rows_ref[piece]
            cols = rows.T
            grow_cols = jnp.exp(cols)
            tail_rows = jnp.exp(rows[:, CH - 1 : CH] - rows)
            ma_ref[offset, 2 * kd :, :] = decay_rows(
                jnp.broadcast_to(jnp.exp(rows[:, CH - 1 : CH]), (8, WIDE))
            )
            for g, key in enumerate(keys):
                k_f = ck[:, head_slice(g)]
                k_b = k_f.astype(BF16)
                key_ref[offset, g] = k_b
                k_t = k_f.T
                rk_col, rk_row = inverse_norms(k_f, 1), inverse_norms(k_t, 0)
                key_dot = dot(k_b, k_t.astype(BF16)) * rk_col * rk_row
                for i in range(2):
                    h = 2 * key + i
                    pair = decay_pairs(rows, cols, h, lower)
                    system = jnp.where(strict, key_dot * pair * cols[:, 4 + h : 5 + h], 0.0)
                    heads.append(
                        dict(
                            out=(ma_ref, solved_ref, offset, 2 * g + i),
                            beta=rows[4 + h : 5 + h],
                            system=system.astype(BF16),
                            inv=halves(unit - system * masks_ref[0].astype(F32)),
                            value=cv[:, head_slice(2 * g + i)].astype(BF16),
                            key=(k_f * (grow_cols[:, h : h + 1] * rk_col)).astype(BF16),
                            tail=halves(k_t * (rk_row * tail_rows[h : h + 1])),
                        )
                    )

    for level in range(1, 7):
        mask = masks_ref[level]
        steps = [dot(p["inv"][0], p["system"] * mask).astype(BF16) for p in heads]
        steps = [halves(dot(s, p["inv"][0])) for s, p in zip(steps, heads)]
        for s, p in zip(steps, heads):
            p["inv"] = (p["inv"][0] - s[0], p["inv"][1] - s[1])

    for p in heads:
        inv = halves((p["inv"][0].astype(F32) + p["inv"][1].astype(F32)) * p["beta"])
        right = jnp.concatenate([p["key"], p["value"]], axis=1)
        p["solved"] = dot(
            jnp.concatenate(inv, axis=1), jnp.concatenate([right, right], axis=0)
        ).astype(BF16)
    for p in heads:
        ma_ref, solved_ref, offset, h = p["out"]
        solved = p["solved"]
        solved_ref[offset, h] = solved
        ma_ref[offset, head_slice(h), :] = dot(
            jnp.concatenate(p["tail"], axis=1), jnp.concatenate([solved, solved], axis=0)
        ).astype(BF16)


def local_call(
    kernel, args, out_shape, scratch=(), flops=100_000_000, vmem_mib=12, scalars=1, name=None
):
    vmem = pl.BlockSpec(memory_space=pltpu.VMEM)
    in_specs = [pl.BlockSpec(memory_space=pltpu.SMEM)] * scalars + [vmem] * (len(args) - scalars)
    return pl.pallas_call(
        kernel,
        out_shape=out_shape,
        in_specs=in_specs,
        out_specs=[vmem] * len(out_shape),
        scratch_shapes=list(scratch),
        cost_estimate=pl.CostEstimate(flops=flops, bytes_accessed=2_000_000, transcendentals=0),
        compiler_params=pltpu.CompilerParams(vmem_limit_bytes=vmem_mib << 20),
        name=name,
    )(*args)


def block_terms(keys, place, shared):
    outs = [
        jax.ShapeDtypeStruct((CHIPS, rows_of(keys), WIDE), BF16),
        jax.ShapeDtypeStruct((CHIPS, 2 * len(keys), CH, WIDE), BF16),
        jax.ShapeDtypeStruct((CHIPS, len(keys), CH, DH), BF16),
    ] * 2
    out = local_call(
        functools.partial(terms_kernel, keys),
        [place, *shared],
        outs,
        [pltpu.VMEM((4 * CHIPS, CH + 8, 2 * len(keys) * DH), F32)],
        vmem_mib=40,
        name="terms",
    )
    return out[:3], out[3:]


def compose_kernel(keys, sc_ref, mine_ref, other_ref, first_ref, *sent_refs):
    count = 2 * len(keys)
    is_first = sc_ref[0] == 0
    for offset in range(CHIPS):
        mine_g, theirs_g = decays_at(mine_ref, offset), decays_at(other_ref, offset)
        first_g = jnp.where(is_first, mine_g, theirs_g)
        second_g = jnp.where(is_first, theirs_g, mine_g)
        first_ref[offset, count * DH :, :] = decay_rows(first_g)
        sent_refs[offset][count * DH :, :] = decay_rows(first_g * second_g)
        for h in range(count):
            mine, theirs = mine_ref[offset, head_slice(h)], other_ref[offset, head_slice(h)]
            first = jnp.where(is_first, mine, theirs)
            second = jnp.where(is_first, theirs, mine)
            first_ref[offset, head_slice(h), :] = first
            product = dot(second[:, :DH], first)
            at = 2 * keys[0] + h
            kept = jnp.concatenate(
                [second[:, :DH].astype(F32) * first_g[at : at + 1, :DH], second[:, DH:].astype(F32)],
                axis=1,
            )
            sent_refs[offset][head_slice(h), :] = (
                first.astype(F32) * second_g[at : at + 1] - product + kept
            ).astype(BF16)


def compose(keys, place, mine, other):
    one = jax.ShapeDtypeStruct((rows_of(keys), WIDE), BF16)
    first, *sent = local_call(
        functools.partial(compose_kernel, keys),
        [place, mine, other],
        [jax.ShapeDtypeStruct(mine.shape, BF16)] + [one] * CHIPS,
        vmem_mib=16,
        name="compose",
    )
    return first, sent


def queries_kernel(keys, mine, sc_ref, x_ref, rim_ref, w_ref, rows_ref, solved_ref, key_ref, *refs):
    loc_ref, car_ref, scr = refs
    owner = sc_ref[0] if mine else 1 - sc_ref[0]
    t_at, s_at = token_order()
    heads = []
    for offset in range(CHIPS):
        piece = owner * (VH // 2 // PIECE) + (sc_ref[1] ^ offset)
        kd = len(keys) * DH
        key_at = piece * PIECE // 2 + keys[0]
        cq = convolved(x_ref, rim_ref, w_ref, scr, offset, key_at * DH, kd)
        rows = rows_ref[piece]
        cols = rows.T
        grow_cols = jnp.exp(cols)
        for g, key in enumerate(keys):
            q_f = cq[:, head_slice(g)]
            k_t = key_ref[offset, g].astype(F32).T
            rq_col = inverse_norms(q_f, 1) * DH ** (-0.5)
            query_dot = dot(q_f.astype(BF16), k_t.astype(BF16)) * rq_col * inverse_norms(k_t, 0)
            for i in range(2):
                h = 2 * key + i
                mixing = halves(query_dot * decay_pairs(rows, cols, h, t_at >= s_at))
                query = q_f * (grow_cols[:, h : h + 1] * rq_col)
                heads.append((offset, 2 * g + i, mixing, query))
    for offset, h, mixing, query in heads:
        solved = solved_ref[offset, h]
        both = dot(jnp.concatenate(mixing, axis=1), jnp.concatenate([solved, solved], axis=0))
        loc_ref[offset, h] = both[:, DH:]
        car_ref[offset, h] = jnp.concatenate(halves(query - both[:, :DH]), axis=1)


def block_queries(keys, mine, place, shared, solved, key_rows):
    count = 2 * len(keys)
    return local_call(
        functools.partial(queries_kernel, keys, mine),
        [place, *shared[:3], shared[4], solved, key_rows],
        [
            jax.ShapeDtypeStruct((CHIPS, count, CH, DH), F32),
            jax.ShapeDtypeStruct((CHIPS, count, CH, WIDE), BF16),
        ],
        [pltpu.VMEM((CHIPS, CH + 8, len(keys) * DH), F32)],
        vmem_mib=24,
        name="queries",
    )


def decays_at(ref, slot):
    return decays_of(ref[slot, ref.shape[1] - 16 :])


def advance(keys, ref, slot, h, decays, state):
    mats = ref[slot, head_slice(h)]
    at = 2 * keys[0] + h
    moved = state.astype(F32) * decays[at : at + 1, :DH] - dot(mats[:, :DH], state)
    return (moved + mats[:, DH:].astype(F32)).astype(BF16)


def gather_kernel(keys, sc_ref, p0, p1, p2, p3, in_ref, order_ref, out_ref):
    for offset, piece in enumerate((p0, p1, p2, p3)):
        order_ref[sc_ref[1] ^ offset] = piece[...]
    states = [in_ref[h] for h in range(2 * len(keys))]
    for chip in range(CHIPS):
        decays = decays_at(order_ref, chip)
        states = [advance(keys, order_ref, chip, h, decays, s) for h, s in enumerate(states)]
    for h, state in enumerate(states):
        out_ref[h] = state


def spread_kernel(keys, sc_ref, order_ref, in_ref, o0, o1, o2, o3, scr):
    states = [in_ref[h] for h in range(2 * len(keys))]
    for chip in range(CHIPS):
        for h, state in enumerate(states):
            scr[chip, h] = state
        if chip < CHIPS - 1:
            decays = decays_at(order_ref, chip)
            states = [advance(keys, order_ref, chip, h, decays, s) for h, s in enumerate(states)]
    for offset, out in enumerate((o0, o1, o2, o3)):
        out[...] = scr[sc_ref[1] ^ offset]


def enter_kernel(keys, sc_ref, first_ref, *refs):
    starts, (keep_ref, send_ref) = refs[:CHIPS], refs[CHIPS:]
    is_first = sc_ref[0] == 0
    for offset in range(CHIPS):
        decays = decays_at(first_ref, offset)
        for h in range(2 * len(keys)):
            start = starts[offset][h]
            after = advance(keys, first_ref, offset, h, decays, start)
            keep_ref[offset, h] = jnp.where(is_first, start, after)
            send_ref[offset, h] = jnp.where(is_first, after, start)


def finish_kernel(mine, sc_ref, gate_ref, gain_ref, *refs):
    bands = [refs[3 * b : 3 * b + 3] for b in range(len(BANDS))]
    out_ref, scr, sems = refs[-3:]
    owner = sc_ref[0] if mine else 1 - sc_ref[0]
    copies = []
    for offset in range(CHIPS):
        piece = owner * (VH // 2 // PIECE) + (sc_ref[1] ^ offset)
        cols = pl.ds(pl.multiple_of(piece * PIECE * DH, PIECE * DH), PIECE * DH)
        gates = gate_ref[:, cols].astype(F32)
        gates = gates / (1.0 + jnp.exp(-gates))
        at = 0
        for state_ref, loc_ref, car_ref in bands:
            for h in range(state_ref.shape[1]):
                state = state_ref[offset, h]
                core = loc_ref[offset, h] + dot(
                    car_ref[offset, h], jnp.concatenate([state, state], axis=0)
                )
                mean_sq = jnp.mean(core * core, axis=1, keepdims=True)
                scaled = core * lax.rsqrt(mean_sq + 1e-06) * gain_ref[...] * gates[:, head_slice(at)]
                scr[offset, :, head_slice(at)] = scaled.astype(BF16)
                at += 1
        copy = pltpu.make_async_copy(scr.at[offset], out_ref.at[:, cols], sems.at[offset])
        copy.start()
        copies.append(copy)
    for copy in copies:
        copy.wait()


def finish(mine, place, gate_in, gain, terms, so_far=None):
    vmem = pl.BlockSpec(memory_space=pltpu.VMEM)
    hbm = pl.BlockSpec(memory_space=pl.ANY)
    args = [place, gate_in, gain, *terms]
    in_specs = [pl.BlockSpec(memory_space=pltpu.SMEM)] + [vmem] * (len(args) - 1)
    aliases = {}
    if so_far is not None:
        aliases = {len(args): 0}
        args.append(so_far)
        in_specs.append(hbm)
    return pl.pallas_call(
        functools.partial(finish_kernel, mine),
        out_shape=jax.ShapeDtypeStruct(gate_in.shape, BF16),
        in_specs=in_specs,
        out_specs=hbm,
        scratch_shapes=[
            pltpu.VMEM((CHIPS, CH, PIECE * DH), BF16),
            pltpu.SemaphoreType.DMA((CHIPS,)),
        ],
        input_output_aliases=aliases,
        cost_estimate=pl.CostEstimate(flops=300_000_000, bytes_accessed=4_000_000, transcendentals=0),
        compiler_params=pltpu.CompilerParams(vmem_limit_bytes=16 << 20),
        name="finish",
    )(*args)


def shift(block, distance):
    count = lax.axis_size("seq")
    return lax.ppermute(block, "seq", [(i, i + distance) for i in range(count - distance)])


def swap(block, distance):
    return lax.ppermute(block, "seq", [(i, i ^ distance) for i in range(lax.axis_size("seq"))])


def level_masks():
    t_at, s_at = np.arange(CH)[:, None], np.arange(CH)[None, :]
    return np.stack(
        [(t_at > s_at) & ((t_at ^ s_at) >> level == 1) for level in range(7)]
    ).astype(ml_dtypes.bfloat16)


def local(mixed_qkv, conv_weight, beta_logit, log_decay, gate_in, norm_gain):
    at = lax.axis_index("seq")
    place = jnp.stack([at % 2, (at // 2) % CHIPS])
    rim = shift(mixed_qkv[CH - 8 :], 1)
    (rows,) = local_call(
        rows_kernel,
        [log_decay.T, beta_logit.T],
        [jax.ShapeDtypeStruct((VH // PIECE, 2 * PIECE, CH), F32)],
        scalars=0,
        name="rows",
    )
    conv_out = early_conv(place[:1], mixed_qkv, conv_weight)
    shared = (mixed_qkv, rim, conv_weight, conv_out, rows, jnp.asarray(level_masks()))
    chips = range(CHIPS)
    finals = [[], []]
    for keys in BANDS:
        theirs, mine = block_terms(keys, place, shared)
        other = swap(theirs[0], 1)
        first, sent = compose(keys, place, mine[0], other)
        pieces = [swap(sent[n], 2 * n) if n else sent[0] for n in chips]
        queries = [
            block_queries(keys, own, place, shared, *part[1:])
            for own, part in ((False, theirs), (True, mine))
        ]
        turn, _ = lax.optimization_barrier((place, queries))

        count = 2 * len(keys)
        state_shape = jax.ShapeDtypeStruct((count, DH, DH), BF16)
        order_shape = jax.ShapeDtypeStruct((CHIPS, rows_of(keys), WIDE), BF16)
        entering = jnp.zeros((count, DH, DH), BF16)
        for _ in range(max(lax.axis_size("seq") // (2 * CHIPS) - 1, 1)):
            order, leaving = local_call(
                functools.partial(gather_kernel, keys),
                [turn, *pieces, entering],
                [order_shape, state_shape],
                name="gather",
            )
            entering = shift(leaving, 2 * CHIPS)
        spread = local_call(
            functools.partial(spread_kernel, keys),
            [place, order, entering],
            [state_shape] * CHIPS,
            [pltpu.VMEM((CHIPS, count, DH, DH), BF16)],
            name="spread",
        )
        starts = [swap(spread[n], 2 * n) if n else spread[0] for n in chips]
        states_shape = jax.ShapeDtypeStruct((CHIPS, count, DH, DH), BF16)
        keep, send = local_call(
            functools.partial(enter_kernel, keys),
            [place, first, *starts],
            [states_shape, states_shape],
            name="enter",
        )
        finals[0] += [swap(send, 1), *queries[0]]
        finals[1] += [keep, *queries[1]]
    gain = norm_gain[None]
    out = finish(True, place, gate_in, gain, finals[1])
    return finish(False, place, gate_in, gain, finals[0], out)


def solution(mesh):
    spec = P(("groups", "seq"), None)
    return jax.shard_map(
        local,
        mesh=mesh,
        in_specs=(spec, P(), spec, spec, spec, P()),
        out_specs=spec,
        check_vma=False,
    )
```

```python
import functools

import jax
import jax.numpy as jnp
import ml_dtypes
import numpy as np
from jax import lax
from jax.experimental import pallas as pl
from jax.experimental.pallas import tpu as pltpu
from jax.sharding import PartitionSpec as P

KH = 16
VH = 32
DH = 128
CH = 128
CHIPS = 4
PIECE = 4
BANDS = ((0,), (1,))
WIDE = 2 * DH

F32 = jnp.float32
BF16 = jnp.bfloat16


def dot(a, b):
    return jnp.dot(a, b, preferred_element_type=F32)


def halves(x):
    high = x.astype(BF16)
    return high, (x - high.astype(F32)).astype(BF16)


def decay_rows(decays):
    high, low = halves(decays)
    return jnp.concatenate([high, low], axis=0)


def rows_of(keys):
    return 2 * len(keys) * DH + 16


def decays_of(rows):
    rows = rows.astype(F32)
    return rows[:8] + rows[8:]


def head_slice(h):
    return slice(h * DH, (h + 1) * DH)


def rows_kernel(decay_ref, logit_ref, rows_ref):
    s_at = lax.broadcasted_iota(jnp.int32, (CH, CH), 0)
    t_at = lax.broadcasted_iota(jnp.int32, (CH, CH), 1)
    cumulative = jnp.dot(
        decay_ref[...],
        (s_at <= t_at).astype(F32),
        precision=lax.Precision.HIGHEST,
        preferred_element_type=F32,
    )
    beta = 1.0 / (1.0 + jnp.exp(-logit_ref[...].astype(F32)))
    for g in range(VH // PIECE):
        rows_ref[g, :PIECE] = cumulative[g * PIECE : (g + 1) * PIECE]
        rows_ref[g, PIECE:] = beta[g * PIECE : (g + 1) * PIECE]


def taps(padded, w, height):
    total = padded(0) * w[0:1]
    for tap in range(1, 4):
        total = total + padded(tap) * w[tap : tap + 1]
    return (total / (1.0 + jnp.exp(-total))).astype(BF16)


def load_kernel(x_ref, w_ref, x_out, w_out, rim_out, sems):
    copies = [
        pltpu.make_async_copy(x_ref.at[CH - 4 :], rim_out, sems.at[0]),
        pltpu.make_async_copy(w_ref, w_out, sems.at[1]),
    ]
    step = CH // 4
    for i in range(4):
        part = pl.ds(i * step, step)
        copies.append(pltpu.make_async_copy(x_ref.at[part], x_out.at[part], sems.at[2 + i]))
    for copy in copies:
        copy.start()
    for copy in copies:
        copy.wait()


def load(mixed_qkv, conv_weight):
    vmem = pl.BlockSpec(memory_space=pltpu.VMEM)
    return pl.pallas_call(
        load_kernel,
        out_shape=[
            jax.ShapeDtypeStruct(mixed_qkv.shape, BF16),
            jax.ShapeDtypeStruct(conv_weight.shape, BF16),
            jax.ShapeDtypeStruct((4, mixed_qkv.shape[1]), BF16),
        ],
        in_specs=[pl.BlockSpec(memory_space=pl.ANY)] * 2,
        out_specs=[vmem] * 3,
        scratch_shapes=[pltpu.SemaphoreType.DMA((6,))],
        cost_estimate=pl.CostEstimate(flops=100, bytes_accessed=100, transcendentals=0),
        compiler_params=pltpu.CompilerParams(vmem_limit_bytes=4 << 20),
        name="load",
    )(*(pltpu.with_memory_space_constraint(a, pltpu.HBM) for a in (mixed_qkv, conv_weight)))


def conv_kernel(sc_ref, x_ref, w_ref, out_ref, scr):
    owner = 1 - sc_ref[0]
    width = scr.shape[2]
    keys, values = KH // 2 * DH // width, VH // 2 * DH // width
    starts = [KH * DH + (owner * keys + i) * width for i in range(keys)]
    starts += [2 * KH * DH + (owner * values + i) * width for i in range(values)]
    for i, start in enumerate(starts):
        cols = pl.ds(pl.multiple_of(start, width), width)
        scr[i % 2] = x_ref[:, cols].astype(F32)
        w = w_ref[:, cols].astype(F32)
        out_ref[8:, cols] = taps(lambda tap: scr[i % 2, 5 + tap : 5 + tap + CH - 8, :], w, CH - 8)


def early_conv(place, x, conv_weight):
    return local_call(
        conv_kernel,
        [place, x, conv_weight],
        [jax.ShapeDtypeStruct(x.shape, BF16)],
        [pltpu.VMEM((2, CH, 512), F32)],
        flops=10_000_000,
        vmem_mib=4,
        name="conv",
    )[0]


def convolved(x_ref, rim_ref, w_ref, scr, slot, column, width, conv_ref=None):
    cols = pl.ds(pl.multiple_of(column, DH), width)
    w = w_ref[:, cols].astype(F32)
    scr[slot, 4:8, :width] = rim_ref[:, cols].astype(F32)
    if conv_ref is None:
        scr[slot, 8 : 8 + CH, :width] = x_ref[:, cols].astype(F32)
        return taps(lambda tap: scr[slot, 5 + tap : 5 + tap + CH, :width], w, CH).astype(F32)
    scr[slot, 8:16, :width] = x_ref[:8, cols].astype(F32)
    first = taps(lambda tap: scr[slot, 5 + tap : 13 + tap, :width], w, 8)
    rest = conv_ref[:, cols].astype(F32)
    return jnp.concatenate([first.astype(F32), rest[8:]], axis=0)


def inverse_norms(rows, axis):
    return lax.rsqrt(jnp.sum(rows * rows, axis=axis, keepdims=True) + 1e-06)


def decay_pairs(rows, cols, h):
    return jnp.exp(jnp.minimum(cols[:, h : h + 1] - rows[h : h + 1], 0.0))


def token_order():
    t_at = lax.broadcasted_iota(jnp.int32, (CH, CH), 0)
    s_at = lax.broadcasted_iota(jnp.int32, (CH, CH), 1)
    return t_at, s_at


def terms_kernel(keys, sc_ref, x_ref, rim_ref, w_ref, conv_ref, rows_ref, masks_ref, *refs):
    theirs_refs, mine_refs, scr = refs[:3], refs[3:6], refs[6]
    t_at, s_at = token_order()
    strict = t_at > s_at
    unit = (t_at == s_at).astype(F32).astype(BF16)
    pieces = VH // 2 // PIECE
    kd, vd = len(keys) * DH, 2 * len(keys) * DH

    heads = []
    slot = 0
    for own, (ma_ref, solved_ref, key_ref) in enumerate((theirs_refs, mine_refs)):
        owner = sc_ref[0] if own else 1 - sc_ref[0]
        conv = functools.partial(
            convolved, x_ref, rim_ref, w_ref, scr, conv_ref=None if own else conv_ref
        )
        for offset in range(CHIPS):
            piece = owner * pieces + (sc_ref[1] ^ offset)
            key_at = piece * PIECE // 2 + keys[0]
            ck = conv(slot, (KH + key_at) * DH, kd)
            cv = conv(slot + 1, 2 * (KH + key_at) * DH, vd)
            slot += 2
            rows = rows_ref[piece]
            cols = rows.T
            grow_cols = jnp.exp(cols)
            tail_rows = jnp.exp(rows[:, CH - 1 : CH] - rows)
            ma_ref[offset, 2 * kd :, :] = decay_rows(
                jnp.broadcast_to(jnp.exp(rows[:, CH - 1 : CH]), (8, WIDE))
            )
            for g, key in enumerate(keys):
                k_f = ck[:, head_slice(g)]
                k_b = k_f.astype(BF16)
                key_ref[offset, g] = k_b
                k_t = k_f.T
                rk_col, rk_row = inverse_norms(k_f, 1), inverse_norms(k_t, 0)
                key_dot = dot(k_b, k_t.astype(BF16)) * rk_col * rk_row
                for i in range(2):
                    h = 2 * key + i
                    system = key_dot * decay_pairs(rows, cols, h)
                    system = jnp.where(strict, system, 0.0).astype(BF16)
                    beta_row = rows[4 + h : 5 + h]
                    gains = (cols[:, 4 + h : 5 + h] * beta_row).astype(BF16)
                    high, low = halves(jnp.broadcast_to(beta_row, (CH, CH)))
                    heads.append(
                        dict(
                            out=(ma_ref, solved_ref, offset, 2 * g + i),
                            system=system,
                            inv=unit * high - system * masks_ref[0] * gains,
                            inv_low=unit * low,
                            value=cv[:, head_slice(2 * g + i)].astype(BF16),
                            key=(k_f * (grow_cols[:, h : h + 1] * rk_col)).astype(BF16),
                            tail=(k_t * (rk_row * tail_rows[h : h + 1])).astype(BF16),
                        )
                    )

    for level in range(1, 7):
        mask = masks_ref[level]
        steps = [dot(p["inv"], p["system"] * mask).astype(BF16) for p in heads]
        steps = [dot(s, p["inv"]).astype(BF16) for s, p in zip(steps, heads)]
        for s, p in zip(steps, heads):
            p["inv"] = p["inv"] - s

    for p in heads:
        right = jnp.concatenate([p["key"], p["value"]], axis=1)
        p["solved"] = dot(
            jnp.concatenate([p["inv"], p["inv_low"]], axis=1),
            jnp.concatenate([right, right], axis=0),
        ).astype(BF16)
    for p in heads:
        ma_ref, solved_ref, offset, h = p["out"]
        solved = p["solved"]
        solved_ref[offset, h] = solved
        ma_ref[offset, head_slice(h), :] = dot(p["tail"], solved).astype(BF16)


def local_call(
    kernel, args, out_shape, scratch=(), flops=100_000_000, vmem_mib=12, scalars=1, name=None
):
    vmem = pl.BlockSpec(memory_space=pltpu.VMEM)
    in_specs = [pl.BlockSpec(memory_space=pltpu.SMEM)] * scalars + [vmem] * (len(args) - scalars)
    return pl.pallas_call(
        kernel,
        out_shape=out_shape,
        in_specs=in_specs,
        out_specs=[vmem] * len(out_shape),
        scratch_shapes=list(scratch),
        cost_estimate=pl.CostEstimate(flops=100, bytes_accessed=100, transcendentals=0),
        compiler_params=pltpu.CompilerParams(vmem_limit_bytes=vmem_mib << 20),
        name=name,
    )(*args)


def block_terms(keys, place, shared):
    outs = [
        jax.ShapeDtypeStruct((CHIPS, rows_of(keys), WIDE), BF16),
        jax.ShapeDtypeStruct((CHIPS, 2 * len(keys), CH, WIDE), BF16),
        jax.ShapeDtypeStruct((CHIPS, len(keys), CH, DH), BF16),
    ] * 2
    out = local_call(
        functools.partial(terms_kernel, keys),
        [place, *shared],
        outs,
        [pltpu.VMEM((4 * CHIPS, CH + 8, 2 * len(keys) * DH), F32)],
        vmem_mib=40,
        name="terms",
    )
    return out[:3], out[3:]


def compose_kernel(keys, sc_ref, mine_ref, other_ref, first_ref, *sent_refs):
    count = 2 * len(keys)
    is_first = sc_ref[0] == 0
    for offset in range(CHIPS):
        mine_g, theirs_g = decays_at(mine_ref, offset), decays_at(other_ref, offset)
        first_g = jnp.where(is_first, mine_g, theirs_g)
        second_g = jnp.where(is_first, theirs_g, mine_g)
        first_ref[offset, count * DH :, :] = decay_rows(first_g)
        sent_refs[offset][count * DH :, :] = decay_rows(first_g * second_g)
        for h in range(count):
            mine, theirs = mine_ref[offset, head_slice(h)], other_ref[offset, head_slice(h)]
            first = jnp.where(is_first, mine, theirs)
            second = jnp.where(is_first, theirs, mine)
            first_ref[offset, head_slice(h), :] = first
            product = dot(second[:, :DH], first)
            at = 2 * keys[0] + h
            kept = jnp.concatenate(
                [second[:, :DH].astype(F32) * first_g[at : at + 1, :DH], second[:, DH:].astype(F32)],
                axis=1,
            )
            sent_refs[offset][head_slice(h), :] = (
                first.astype(F32) * second_g[at : at + 1] - product + kept
            ).astype(BF16)


def compose(keys, place, mine, other):
    one = jax.ShapeDtypeStruct((rows_of(keys), WIDE), BF16)
    first, *sent = local_call(
        functools.partial(compose_kernel, keys),
        [place, mine, other],
        [jax.ShapeDtypeStruct(mine.shape, BF16)] + [one] * CHIPS,
        vmem_mib=16,
        name="compose",
    )
    return first, sent


def queries_kernel(keys, mine, sc_ref, x_ref, rim_ref, w_ref, rows_ref, solved_ref, key_ref, *refs):
    loc_ref, car_ref, scr = refs
    owner = sc_ref[0] if mine else 1 - sc_ref[0]
    t_at, s_at = token_order()
    heads = []
    for offset in range(CHIPS):
        piece = owner * (VH // 2 // PIECE) + (sc_ref[1] ^ offset)
        kd = len(keys) * DH
        key_at = piece * PIECE // 2 + keys[0]
        cq = convolved(x_ref, rim_ref, w_ref, scr, offset, key_at * DH, kd)
        rows = rows_ref[piece]
        cols = rows.T
        grow_cols = jnp.exp(cols)
        for g, key in enumerate(keys):
            q_f = cq[:, head_slice(g)]
            k_t = key_ref[offset, g].astype(F32).T
            rq_col = inverse_norms(q_f, 1) * DH ** (-0.5)
            query_dot = dot(q_f.astype(BF16), k_t.astype(BF16)) * rq_col * inverse_norms(k_t, 0)
            for i in range(2):
                h = 2 * key + i
                mixing = query_dot * decay_pairs(rows, cols, h)
                mixing = halves(jnp.where(t_at >= s_at, mixing, 0.0))
                query = q_f * (grow_cols[:, h : h + 1] * rq_col)
                heads.append((offset, 2 * g + i, mixing, query))
    for offset, h, mixing, query in heads:
        solved = solved_ref[offset, h]
        both = dot(jnp.concatenate(mixing, axis=1), jnp.concatenate([solved, solved], axis=0))
        loc_ref[offset, h] = both[:, DH:]
        car_ref[offset, h] = (query - both[:, :DH]).astype(BF16)


def block_queries(keys, mine, place, shared, solved, key_rows):
    count = 2 * len(keys)
    return local_call(
        functools.partial(queries_kernel, keys, mine),
        [place, *shared[:3], shared[4], solved, key_rows],
        [
            jax.ShapeDtypeStruct((CHIPS, count, CH, DH), F32),
            jax.ShapeDtypeStruct((CHIPS, count, CH, DH), BF16),
        ],
        [pltpu.VMEM((CHIPS, CH + 8, len(keys) * DH), F32)],
        vmem_mib=24,
        name="queries",
    )


def decays_at(ref, slot):
    return decays_of(ref[slot, ref.shape[1] - 16 :])


def advance(keys, ref, slot, h, decays, state):
    mats = ref[slot, head_slice(h)]
    at = 2 * keys[0] + h
    moved = state.astype(F32) * decays[at : at + 1, :DH] - dot(mats[:, :DH], state)
    return (moved + mats[:, DH:].astype(F32)).astype(BF16)


def gather_kernel(keys, sc_ref, p0, p1, p2, p3, in_ref, order_ref, out_ref):
    for offset, piece in enumerate((p0, p1, p2, p3)):
        order_ref[sc_ref[1] ^ offset] = piece[...]
    states = [in_ref[h] for h in range(2 * len(keys))]
    for chip in range(CHIPS):
        decays = decays_at(order_ref, chip)
        states = [advance(keys, order_ref, chip, h, decays, s) for h, s in enumerate(states)]
    for h, state in enumerate(states):
        out_ref[h] = state


def spread_kernel(keys, sc_ref, order_ref, in_ref, o0, o1, o2, o3, scr):
    states = [in_ref[h] for h in range(2 * len(keys))]
    for chip in range(CHIPS):
        for h, state in enumerate(states):
            scr[chip, h] = state
        if chip < CHIPS - 1:
            decays = decays_at(order_ref, chip)
            states = [advance(keys, order_ref, chip, h, decays, s) for h, s in enumerate(states)]
    for offset, out in enumerate((o0, o1, o2, o3)):
        out[...] = scr[sc_ref[1] ^ offset]


def enter_kernel(keys, sc_ref, first_ref, *refs):
    starts, (keep_ref, send_ref) = refs[:CHIPS], refs[CHIPS:]
    is_first = sc_ref[0] == 0
    for offset in range(CHIPS):
        decays = decays_at(first_ref, offset)
        for h in range(2 * len(keys)):
            start = starts[offset][h]
            after = advance(keys, first_ref, offset, h, decays, start)
            keep_ref[offset, h] = jnp.where(is_first, start, after)
            send_ref[offset, h] = jnp.where(is_first, after, start)


def piece_columns(own, sc_ref, offset):
    owner = sc_ref[0] if own else 1 - sc_ref[0]
    piece = owner * (VH // 2 // PIECE) + (sc_ref[1] ^ offset)
    return pl.ds(pl.multiple_of(piece * PIECE * DH, PIECE * DH), PIECE * DH)


def finish_piece(own, offset, sc_ref, gate_ref, gain_ref, bands, out_ref):
    gates = gate_ref[:, piece_columns(own, sc_ref, offset)].astype(F32)
    gates = gates / (1.0 + jnp.exp(-gates))
    for keys, (state_ref, loc_ref, car_ref) in zip(BANDS, bands):
        for h in range(2 * len(keys)):
            core = loc_ref[offset, h] + dot(car_ref[offset, h], state_ref[offset, h])
            mean_sq = jnp.mean(core * core, axis=1, keepdims=True)
            cols = head_slice(2 * keys[0] + h)
            scaled = core * lax.rsqrt(mean_sq + 1e-06) * gain_ref[...] * gates[:, cols]
            out_ref[offset, :, cols] = scaled.astype(BF16)


def finish_kernel(sc_ref, gate_ref, gain_ref, *refs):
    bands = [refs[3 * b : 3 * b + 3] for b in range(len(BANDS))]
    for offset in range(CHIPS):
        finish_piece(1, offset, sc_ref, gate_ref, gain_ref, bands, refs[-1])


def finish(place, gate_in, gain, terms):
    return local_call(
        finish_kernel,
        [place, gate_in, gain, *terms],
        [jax.ShapeDtypeStruct((CHIPS, CH, PIECE * DH), BF16)],
        vmem_mib=4,
        name="finish",
    )[0]


def last_kernel(sc_ref, gate_ref, gain_ref, done_ref, *refs):
    bands = [refs[3 * b : 3 * b + 3] for b in range(len(BANDS))]
    out_ref, scr, sems = refs[-3:]
    copies = []

    def send(own, source_ref, offset):
        cols = piece_columns(own, sc_ref, offset)
        copies.append(
            pltpu.make_async_copy(source_ref.at[offset], out_ref.at[:, cols], sems.at[len(copies)])
        )
        copies[-1].start()

    for offset in range(CHIPS):
        send(1, done_ref, offset)
    for offset in range(CHIPS):
        finish_piece(0, offset, sc_ref, gate_ref, gain_ref, bands, scr)
        send(0, scr, offset)
    for copy in copies:
        copy.wait()


def finish_last(place, gate_in, gain, done, terms):
    vmem = pl.BlockSpec(memory_space=pltpu.VMEM)
    args = [place, gate_in, gain, done, *terms]
    return pl.pallas_call(
        last_kernel,
        out_shape=jax.ShapeDtypeStruct(gate_in.shape, BF16),
        in_specs=[pl.BlockSpec(memory_space=pltpu.SMEM)] + [vmem] * (len(args) - 1),
        out_specs=pl.BlockSpec(memory_space=pl.ANY),
        scratch_shapes=[
            pltpu.VMEM((CHIPS, CH, PIECE * DH), BF16),
            pltpu.SemaphoreType.DMA((2 * CHIPS,)),
        ],
        cost_estimate=pl.CostEstimate(flops=100, bytes_accessed=100, transcendentals=0),
        compiler_params=pltpu.CompilerParams(vmem_limit_bytes=4 << 20),
        name="finish_last",
    )(*args)


def shift(block, distance):
    count = lax.axis_size("seq")
    return lax.ppermute(block, "seq", [(i, i + distance) for i in range(count - distance)])


def swap(block, distance):
    return lax.ppermute(block, "seq", [(i, i ^ distance) for i in range(lax.axis_size("seq"))])


def level_masks():
    t_at, s_at = np.arange(CH)[:, None], np.arange(CH)[None, :]
    return np.stack(
        [(t_at > s_at) & ((t_at ^ s_at) >> level == 1) for level in range(7)]
    ).astype(ml_dtypes.bfloat16)


def local(mixed_qkv, conv_weight, beta_logit, log_decay, gate_in, norm_gain):
    at = lax.axis_index("seq")
    place = jnp.stack([at % 2, (at // 2) % CHIPS])
    x, weight, last_rows = load(mixed_qkv, conv_weight)
    rim = shift(last_rows, 1)
    (rows,) = local_call(
        rows_kernel,
        [log_decay.T, beta_logit.T],
        [jax.ShapeDtypeStruct((VH // PIECE, 2 * PIECE, CH), F32)],
        scalars=0,
        name="rows",
    )
    conv_out = early_conv(place, x, weight)
    shared = (x, rim, weight, conv_out, rows, jnp.asarray(level_masks()))
    chips = range(CHIPS)
    finals = [[], []]
    for keys in BANDS:
        theirs, mine = block_terms(keys, place, shared)
        other = swap(theirs[0], 1)
        first, sent = compose(keys, place, mine[0], other)
        pieces = [swap(sent[n], 2 * n) if n else sent[0] for n in range(CHIPS)]
        queries = [
            block_queries(keys, own, place, shared, *part[1:])
            for own, part in enumerate((theirs, mine))
        ]
        turn, _ = lax.optimization_barrier((place, queries))

        count = 2 * len(keys)
        state_shape = jax.ShapeDtypeStruct((count, DH, DH), BF16)
        order_shape = jax.ShapeDtypeStruct((CHIPS, rows_of(keys), WIDE), BF16)
        entering = jnp.zeros((count, DH, DH), BF16)
        for _ in range(max(lax.axis_size("seq") // (2 * CHIPS) - 1, 1)):
            order, leaving = local_call(
                functools.partial(gather_kernel, keys),
                [turn, *pieces, entering],
                [order_shape, state_shape],
                name="gather",
            )
            entering = shift(leaving, 2 * CHIPS)
        spread = local_call(
            functools.partial(spread_kernel, keys),
            [place, order, entering],
            [state_shape] * CHIPS,
            [pltpu.VMEM((CHIPS, count, DH, DH), BF16)],
            name="spread",
        )
        starts = [swap(spread[n], 2 * n) if n else spread[0] for n in range(CHIPS)]
        states_shape = jax.ShapeDtypeStruct((CHIPS, count, DH, DH), BF16)
        keep, send = local_call(
            functools.partial(enter_kernel, keys),
            [place, first, *starts],
            [states_shape, states_shape],
            name="enter",
        )
        for own, state in enumerate((swap(send, 1), keep)):
            finals[own] += [state, *queries[own]]
    gain = norm_gain[None]
    done = finish(place, gate_in, gain, finals[1])
    return finish_last(place, gate_in, gain, done, finals[0])


def solution(mesh):
    spec = P(("groups", "seq"), None)
    return jax.shard_map(
        local,
        mesh=mesh,
        in_specs=(spec, P(), spec, spec, spec, P()),
        out_specs=spec,
        check_vma=False,
    )
```

```python
import functools

import jax
import jax.numpy as jnp
import ml_dtypes
import numpy as np
from jax import lax
from jax.experimental import pallas as pl
from jax.experimental.pallas import tpu as pltpu
from jax.sharding import PartitionSpec as P

KH = 16
VH = 32
DH = 128
CH = 128
CHIPS = 4
PIECE = 4
BANDS = ((0,), (1,))
WIDE = 2 * DH

F32 = jnp.float32
BF16 = jnp.bfloat16


def dot(a, b):
    return jnp.dot(a, b, preferred_element_type=F32)


def halves(x):
    high = x.astype(BF16)
    return high, (x - high.astype(F32)).astype(BF16)


def decay_rows(decays):
    high, low = halves(decays)
    return jnp.concatenate([high, low], axis=0)


def rows_of(keys):
    return 2 * len(keys) * DH + 16


def decays_of(rows):
    rows = rows.astype(F32)
    return rows[:8] + rows[8:]


def head_slice(h):
    return slice(h * DH, (h + 1) * DH)


def rows_kernel(decay_ref, logit_ref, rows_ref):
    s_at = lax.broadcasted_iota(jnp.int32, (CH, CH), 0)
    t_at = lax.broadcasted_iota(jnp.int32, (CH, CH), 1)
    cumulative = jnp.dot(
        decay_ref[...],
        (s_at <= t_at).astype(F32),
        precision=lax.Precision.HIGHEST,
        preferred_element_type=F32,
    )
    beta = 1.0 / (1.0 + jnp.exp(-logit_ref[...].astype(F32)))
    for g in range(VH // PIECE):
        rows_ref[g, :PIECE] = cumulative[g * PIECE : (g + 1) * PIECE]
        rows_ref[g, PIECE:] = beta[g * PIECE : (g + 1) * PIECE]


def taps(padded, w, height):
    total = padded(0) * w[0:1]
    for tap in range(1, 4):
        total = total + padded(tap) * w[tap : tap + 1]
    return (total / (1.0 + jnp.exp(-total))).astype(BF16)


def load_kernel(x_ref, w_ref, x_out, w_out, rim_out, sems):
    copies = [
        pltpu.make_async_copy(x_ref.at[CH - 4 :], rim_out, sems.at[0]),
        pltpu.make_async_copy(w_ref, w_out, sems.at[1]),
    ]
    step = CH // 4
    for i in range(4):
        part = pl.ds(i * step, step)
        copies.append(pltpu.make_async_copy(x_ref.at[part], x_out.at[part], sems.at[2 + i]))
    for copy in copies:
        copy.start()
    for copy in copies:
        copy.wait()


def load(mixed_qkv, conv_weight):
    vmem = pl.BlockSpec(memory_space=pltpu.VMEM)
    return pl.pallas_call(
        load_kernel,
        out_shape=[
            jax.ShapeDtypeStruct(mixed_qkv.shape, BF16),
            jax.ShapeDtypeStruct(conv_weight.shape, BF16),
            jax.ShapeDtypeStruct((4, mixed_qkv.shape[1]), BF16),
        ],
        in_specs=[pl.BlockSpec(memory_space=pl.ANY)] * 2,
        out_specs=[vmem] * 3,
        scratch_shapes=[pltpu.SemaphoreType.DMA((6,))],
        cost_estimate=pl.CostEstimate(flops=100, bytes_accessed=100, transcendentals=0),
        compiler_params=pltpu.CompilerParams(vmem_limit_bytes=4 << 20),
        name="load",
    )(*(pltpu.with_memory_space_constraint(a, pltpu.HBM) for a in (mixed_qkv, conv_weight)))


def conv_kernel(sc_ref, x_ref, w_ref, out_ref, scr):
    owner = 1 - sc_ref[0]
    width = scr.shape[2]
    keys, values = KH // 2 * DH // width, VH // 2 * DH // width
    starts = [KH * DH + (owner * keys + i) * width for i in range(keys)]
    starts += [2 * KH * DH + (owner * values + i) * width for i in range(values)]
    for i, start in enumerate(starts):
        cols = pl.ds(pl.multiple_of(start, width), width)
        scr[i % 2] = x_ref[:, cols].astype(F32)
        w = w_ref[:, cols].astype(F32)
        out_ref[8:, cols] = taps(lambda tap: scr[i % 2, 5 + tap : 5 + tap + CH - 8, :], w, CH - 8)


def early_conv(place, x, conv_weight):
    return local_call(
        conv_kernel,
        [place, x, conv_weight],
        [jax.ShapeDtypeStruct(x.shape, BF16)],
        [pltpu.VMEM((2, CH, 512), F32)],
        flops=10_000_000,
        vmem_mib=4,
        name="conv",
    )[0]


def convolved(x_ref, rim_ref, w_ref, scr, slot, column, width, conv_ref=None):
    cols = pl.ds(pl.multiple_of(column, DH), width)
    w = w_ref[:, cols].astype(F32)
    scr[slot, 4:8, :width] = rim_ref[:, cols].astype(F32)
    if conv_ref is None:
        scr[slot, 8 : 8 + CH, :width] = x_ref[:, cols].astype(F32)
        return taps(lambda tap: scr[slot, 5 + tap : 5 + tap + CH, :width], w, CH).astype(F32)
    scr[slot, 8:16, :width] = x_ref[:8, cols].astype(F32)
    first = taps(lambda tap: scr[slot, 5 + tap : 13 + tap, :width], w, 8)
    rest = conv_ref[:, cols].astype(F32)
    return jnp.concatenate([first.astype(F32), rest[8:]], axis=0)


def inverse_norms(rows, axis):
    return lax.rsqrt(jnp.sum(rows * rows, axis=axis, keepdims=True) + 1e-06)


def decay_pairs(rows, cols, h):
    return jnp.exp(jnp.minimum(cols[:, h : h + 1] - rows[h : h + 1], 0.0))


def token_order():
    t_at = lax.broadcasted_iota(jnp.int32, (CH, CH), 0)
    s_at = lax.broadcasted_iota(jnp.int32, (CH, CH), 1)
    return t_at, s_at


def terms_kernel(keys, sc_ref, x_ref, rim_ref, w_ref, conv_ref, rows_ref, masks_ref, *refs):
    theirs_refs, mine_refs, scr = refs[:3], refs[3:6], refs[6]
    t_at, s_at = token_order()
    strict = t_at > s_at
    unit = (t_at == s_at).astype(F32).astype(BF16)
    pieces = VH // 2 // PIECE
    kd, vd = len(keys) * DH, 2 * len(keys) * DH

    heads = []
    slot = 0
    for own, (ma_ref, solved_ref, key_ref) in enumerate((theirs_refs, mine_refs)):
        owner = sc_ref[0] if own else 1 - sc_ref[0]
        conv = functools.partial(
            convolved, x_ref, rim_ref, w_ref, scr, conv_ref=None if own else conv_ref
        )
        for offset in range(CHIPS):
            piece = owner * pieces + (sc_ref[1] ^ offset)
            key_at = piece * PIECE // 2 + keys[0]
            ck = conv(slot, (KH + key_at) * DH, kd)
            cv = conv(slot + 1, 2 * (KH + key_at) * DH, vd)
            slot += 2
            rows = rows_ref[piece]
            following = pltpu.roll(rows, CH - 1, axis=1)
            cols = rows.T
            grow_cols = jnp.exp(cols)
            tail_rows = jnp.exp(rows[:, CH - 1 : CH] - rows)
            ma_ref[offset, 2 * kd :, :] = decay_rows(
                jnp.broadcast_to(jnp.exp(rows[:, CH - 1 : CH]), (8, WIDE))
            )
            for g, key in enumerate(keys):
                k_f = ck[:, head_slice(g)]
                k_b = k_f.astype(BF16)
                key_ref[offset, g] = k_b
                k_t = k_f.T
                rk_col, rk_row = inverse_norms(k_f, 1), inverse_norms(k_t, 0)
                key_dot = dot(k_b, k_t.astype(BF16)) * rk_col * rk_row
                for i in range(2):
                    h = 2 * key + i
                    system = key_dot * decay_pairs(rows, cols, h)
                    system = jnp.where(strict, system, 0.0).astype(BF16)
                    beta_row = rows[4 + h : 5 + h]
                    gains = jnp.broadcast_to(beta_row * following[4 + h : 5 + h], (CH, CH)).astype(BF16)
                    high, low = halves(jnp.broadcast_to(beta_row, (CH, CH)))
                    heads.append(
                        dict(
                            out=(ma_ref, solved_ref, offset, 2 * g + i),
                            system=system,
                            inv=unit * high - system * masks_ref[0] * gains,
                            inv_low=unit * low,
                            value=cv[:, head_slice(2 * g + i)].astype(BF16),
                            key=(k_f * (grow_cols[:, h : h + 1] * rk_col)).astype(BF16),
                            tail=(k_t * (rk_row * tail_rows[h : h + 1])).astype(BF16),
                        )
                    )

    for level in range(1, 7):
        mask = masks_ref[level]
        steps = [dot(p["inv"], p["system"] * mask).astype(BF16) for p in heads]
        steps = [dot(s, p["inv"]).astype(BF16) for s, p in zip(steps, heads)]
        for s, p in zip(steps, heads):
            p["inv"] = p["inv"] - s

    for p in heads:
        right = jnp.concatenate([p["key"], p["value"]], axis=1)
        p["solved"] = dot(
            jnp.concatenate([p["inv"], p["inv_low"]], axis=1),
            jnp.concatenate([right, right], axis=0),
        ).astype(BF16)
    for p in heads:
        ma_ref, solved_ref, offset, h = p["out"]
        solved = p["solved"]
        solved_ref[offset, h] = solved
        ma_ref[offset, head_slice(h), :] = dot(p["tail"], solved).astype(BF16)


def local_call(
    kernel, args, out_shape, scratch=(), flops=100_000_000, vmem_mib=12, scalars=1, name=None
):
    vmem = pl.BlockSpec(memory_space=pltpu.VMEM)
    in_specs = [pl.BlockSpec(memory_space=pltpu.SMEM)] * scalars + [vmem] * (len(args) - scalars)
    return pl.pallas_call(
        kernel,
        out_shape=out_shape,
        in_specs=in_specs,
        out_specs=[vmem] * len(out_shape),
        scratch_shapes=list(scratch),
        cost_estimate=pl.CostEstimate(flops=100, bytes_accessed=100, transcendentals=0),
        compiler_params=pltpu.CompilerParams(vmem_limit_bytes=vmem_mib << 20),
        name=name,
    )(*args)


def block_terms(keys, place, shared):
    outs = [
        jax.ShapeDtypeStruct((CHIPS, rows_of(keys), WIDE), BF16),
        jax.ShapeDtypeStruct((CHIPS, 2 * len(keys), CH, WIDE), BF16),
        jax.ShapeDtypeStruct((CHIPS, len(keys), CH, DH), BF16),
    ] * 2
    out = local_call(
        functools.partial(terms_kernel, keys),
        [place, *shared],
        outs,
        [pltpu.VMEM((4 * CHIPS, CH + 8, 2 * len(keys) * DH), F32)],
        vmem_mib=40,
        name="terms",
    )
    return out[:3], out[3:]


def compose_kernel(keys, sc_ref, mine_ref, other_ref, first_ref, *sent_refs):
    count = 2 * len(keys)
    is_first = sc_ref[0] == 0
    for offset in range(CHIPS):
        mine_g, theirs_g = decays_at(mine_ref, offset), decays_at(other_ref, offset)
        first_g = jnp.where(is_first, mine_g, theirs_g)
        second_g = jnp.where(is_first, theirs_g, mine_g)
        first_ref[offset, count * DH :, :] = decay_rows(first_g)
        sent_refs[offset][count * DH :, :] = decay_rows(first_g * second_g)
        for h in range(count):
            mine, theirs = mine_ref[offset, head_slice(h)], other_ref[offset, head_slice(h)]
            first = jnp.where(is_first, mine, theirs)
            second = jnp.where(is_first, theirs, mine)
            first_ref[offset, head_slice(h), :] = first
            product = dot(second[:, :DH], first)
            at = 2 * keys[0] + h
            kept = jnp.concatenate(
                [second[:, :DH].astype(F32) * first_g[at : at + 1, :DH], second[:, DH:].astype(F32)],
                axis=1,
            )
            sent_refs[offset][head_slice(h), :] = (
                first.astype(F32) * second_g[at : at + 1] - product + kept
            ).astype(BF16)


def compose(keys, place, mine, other):
    one = jax.ShapeDtypeStruct((rows_of(keys), WIDE), BF16)
    first, *sent = local_call(
        functools.partial(compose_kernel, keys),
        [place, mine, other],
        [jax.ShapeDtypeStruct(mine.shape, BF16)] + [one] * CHIPS,
        vmem_mib=16,
        name="compose",
    )
    return first, sent


def queries_kernel(keys, sc_ref, x_ref, rim_ref, w_ref, rows_ref, *refs):
    ins, outs, scr = (refs[0:2], refs[2:4]), (refs[4:6], refs[6:8]), refs[8]
    t_at, s_at = token_order()
    heads = []
    for own, ((solved_ref, key_ref), out) in enumerate(zip(ins, outs)):
        owner = sc_ref[0] if own else 1 - sc_ref[0]
        for offset in range(CHIPS):
            piece = owner * (VH // 2 // PIECE) + (sc_ref[1] ^ offset)
            kd = len(keys) * DH
            key_at = piece * PIECE // 2 + keys[0]
            cq = convolved(x_ref, rim_ref, w_ref, scr, own * CHIPS + offset, key_at * DH, kd)
            rows = rows_ref[piece]
            cols = rows.T
            grow_cols = jnp.exp(cols)
            for g, key in enumerate(keys):
                q_f = cq[:, head_slice(g)]
                k_t = key_ref[offset, g].astype(F32).T
                rq_col = inverse_norms(q_f, 1) * DH ** (-0.5)
                query_dot = dot(q_f.astype(BF16), k_t.astype(BF16)) * rq_col * inverse_norms(k_t, 0)
                for i in range(2):
                    h = 2 * key + i
                    mixing = query_dot * decay_pairs(rows, cols, h)
                    mixing = halves(jnp.where(t_at >= s_at, mixing, 0.0))
                    query = q_f * (grow_cols[:, h : h + 1] * rq_col)
                    heads.append((solved_ref, out, offset, 2 * g + i, mixing, query))
    for solved_ref, (loc_ref, car_ref), offset, h, mixing, query in heads:
        solved = solved_ref[offset, h]
        both = dot(jnp.concatenate(mixing, axis=1), jnp.concatenate([solved, solved], axis=0))
        loc_ref[offset, h] = both[:, DH:]
        car_ref[offset, h] = (query - both[:, :DH]).astype(BF16)


def block_queries(keys, place, shared, theirs, mine):
    count = 2 * len(keys)
    out = local_call(
        functools.partial(queries_kernel, keys),
        [place, *shared[:3], shared[4], *theirs, *mine],
        [
            jax.ShapeDtypeStruct((CHIPS, count, CH, DH), F32),
            jax.ShapeDtypeStruct((CHIPS, count, CH, DH), BF16),
        ]
        * 2,
        [pltpu.VMEM((2 * CHIPS, CH + 8, len(keys) * DH), F32)],
        vmem_mib=24,
        name="queries",
    )
    return out[:2], out[2:]


def decays_at(ref, slot):
    return decays_of(ref[slot, ref.shape[1] - 16 :])


def advance(keys, ref, slot, h, decays, state):
    mats = ref[slot, head_slice(h)]
    at = 2 * keys[0] + h
    moved = state.astype(F32) * decays[at : at + 1, :DH] - dot(mats[:, :DH], state)
    return (moved + mats[:, DH:].astype(F32)).astype(BF16)


def gather_kernel(keys, sc_ref, p0, p1, p2, p3, in_ref, order_ref, out_ref):
    for offset, piece in enumerate((p0, p1, p2, p3)):
        order_ref[sc_ref[1] ^ offset] = piece[...]

    @pl.when(sc_ref[2] == 0)
    def _():
        states = [in_ref[h] for h in range(2 * len(keys))]
        for chip in range(CHIPS):
            decays = decays_at(order_ref, chip)
            states = [advance(keys, order_ref, chip, h, decays, s) for h, s in enumerate(states)]
        for h, state in enumerate(states):
            out_ref[h] = state

    @pl.when(sc_ref[2] == 1)
    def _():
        out_ref[...] = jnp.zeros_like(out_ref)


def spread_kernel(keys, sc_ref, order_ref, in_ref, o0, o1, o2, o3, scr):
    states = [in_ref[h] for h in range(2 * len(keys))]
    for chip in range(CHIPS):
        for h, state in enumerate(states):
            scr[chip, h] = state
        if chip < CHIPS - 1:
            decays = decays_at(order_ref, chip)
            states = [advance(keys, order_ref, chip, h, decays, s) for h, s in enumerate(states)]
    for offset, out in enumerate((o0, o1, o2, o3)):
        out[...] = scr[sc_ref[1] ^ offset]


def enter_kernel(keys, sc_ref, first_ref, *refs):
    starts, (keep_ref, send_ref) = refs[:CHIPS], refs[CHIPS:]
    is_first = sc_ref[0] == 0
    for offset in range(CHIPS):
        decays = decays_at(first_ref, offset)
        for h in range(2 * len(keys)):
            start = starts[offset][h]
            after = advance(keys, first_ref, offset, h, decays, start)
            keep_ref[offset, h] = jnp.where(is_first, start, after)
            send_ref[offset, h] = jnp.where(is_first, after, start)


def gates_kernel(gate_ref, gain_ref, out_ref):
    gates = gate_ref[...].astype(F32)
    gates = gates / (1.0 + jnp.exp(-gates))
    for h in range(VH):
        out_ref[:, head_slice(h)] = gates[:, head_slice(h)] * gain_ref[...]


def piece_columns(own, sc_ref, offset):
    owner = sc_ref[0] if own else 1 - sc_ref[0]
    piece = owner * (VH // 2 // PIECE) + (sc_ref[1] ^ offset)
    return pl.ds(pl.multiple_of(piece * PIECE * DH, PIECE * DH), PIECE * DH)


def finish_piece(own, offset, sc_ref, gate_ref, bands, out_ref):
    gates = gate_ref[:, piece_columns(own, sc_ref, offset)]
    for keys, (state_ref, loc_ref, car_ref) in zip(BANDS, bands):
        for h in range(2 * len(keys)):
            core = loc_ref[offset, h] + dot(car_ref[offset, h], state_ref[offset, h])
            mean_sq = jnp.mean(core * core, axis=1, keepdims=True)
            cols = head_slice(2 * keys[0] + h)
            scaled = core * lax.rsqrt(mean_sq + 1e-06) * gates[:, cols]
            out_ref[offset, :, cols] = scaled.astype(BF16)


def finish_kernel(sc_ref, gate_ref, *refs):
    bands = [refs[3 * b : 3 * b + 3] for b in range(len(BANDS))]
    for offset in range(CHIPS):
        finish_piece(1, offset, sc_ref, gate_ref, bands, refs[-1])


def finish(place, gates, terms):
    return local_call(
        finish_kernel,
        [place, gates, *terms],
        [jax.ShapeDtypeStruct((CHIPS, CH, PIECE * DH), BF16)],
        vmem_mib=4,
        name="finish",
    )[0]


def last_kernel(sc_ref, gate_ref, done_ref, *refs):
    bands = [refs[3 * b : 3 * b + 3] for b in range(len(BANDS))]
    out_ref, scr, sems = refs[-3:]
    copies = []

    def send(own, source_ref, offset):
        cols = piece_columns(own, sc_ref, offset)
        copies.append(
            pltpu.make_async_copy(source_ref.at[offset], out_ref.at[:, cols], sems.at[len(copies)])
        )
        copies[-1].start()

    for offset in range(CHIPS):
        send(1, done_ref, offset)
    for offset in range(CHIPS):
        finish_piece(0, offset, sc_ref, gate_ref, bands, scr)
        send(0, scr, offset)
    for copy in copies:
        copy.wait()


def finish_last(place, gates, done, terms):
    vmem = pl.BlockSpec(memory_space=pltpu.VMEM)
    args = [place, gates, done, *terms]
    return pl.pallas_call(
        last_kernel,
        out_shape=jax.ShapeDtypeStruct(gates.shape, BF16),
        in_specs=[pl.BlockSpec(memory_space=pltpu.SMEM)] + [vmem] * (len(args) - 1),
        out_specs=pl.BlockSpec(memory_space=pl.ANY),
        scratch_shapes=[
            pltpu.VMEM((CHIPS, CH, PIECE * DH), BF16),
            pltpu.SemaphoreType.DMA((2 * CHIPS,)),
        ],
        cost_estimate=pl.CostEstimate(flops=100, bytes_accessed=100, transcendentals=0),
        compiler_params=pltpu.CompilerParams(vmem_limit_bytes=4 << 20),
        name="finish_last",
    )(*args)


def shift(block, distance):
    count = lax.axis_size("seq")
    return lax.ppermute(block, "seq", [(i, i + distance) for i in range(count - distance)])


def swap(block, distance):
    return lax.ppermute(block, "seq", [(i, i ^ distance) for i in range(lax.axis_size("seq"))])


def level_masks():
    t_at, s_at = np.arange(CH)[:, None], np.arange(CH)[None, :]
    return np.stack(
        [(t_at > s_at) & ((t_at ^ s_at) >> level == 1) for level in range(7)]
    ).astype(ml_dtypes.bfloat16)


def local(mixed_qkv, conv_weight, beta_logit, log_decay, gate_in, norm_gain):
    at = lax.axis_index("seq")
    last = at // (2 * CHIPS) == lax.axis_size("seq") // (2 * CHIPS) - 1
    place = jnp.stack([at % 2, (at // 2) % CHIPS, last.astype(at.dtype)])
    x, weight, last_rows = load(mixed_qkv, conv_weight)
    rim = shift(last_rows, 1)
    (rows,) = local_call(
        rows_kernel,
        [log_decay.T, beta_logit.T],
        [jax.ShapeDtypeStruct((VH // PIECE, 2 * PIECE, CH), F32)],
        scalars=0,
        name="rows",
    )
    conv_out = early_conv(place, x, weight)
    shared = (x, rim, weight, conv_out, rows, jnp.asarray(level_masks()))
    chips = range(CHIPS)
    finals = [[], []]
    (gates,) = local_call(
        gates_kernel,
        [gate_in, norm_gain[None]],
        [jax.ShapeDtypeStruct(gate_in.shape, F32)],
        scalars=0,
        vmem_mib=4,
        name="gates",
    )
    for keys in BANDS:
        theirs, mine = block_terms(keys, place, shared)
        other = swap(theirs[0], 1)
        first, sent = compose(keys, place, mine[0], other)
        pieces = [swap(sent[n], 2 * n) if n else sent[0] for n in range(CHIPS)]
        queries = block_queries(keys, place, shared, theirs[1:], mine[1:])
        turn, _ = lax.optimization_barrier((place, queries))

        count = 2 * len(keys)
        state_shape = jax.ShapeDtypeStruct((count, DH, DH), BF16)
        order_shape = jax.ShapeDtypeStruct((CHIPS, rows_of(keys), WIDE), BF16)
        entering = jnp.zeros((count, DH, DH), BF16)
        for _ in range(max(lax.axis_size("seq") // (2 * CHIPS) - 1, 1)):
            order, leaving = local_call(
                functools.partial(gather_kernel, keys),
                [turn, *pieces, entering],
                [order_shape, state_shape],
                name="gather",
            )
            entering = shift(leaving, 2 * CHIPS)
        spread = local_call(
            functools.partial(spread_kernel, keys),
            [place, order, entering],
            [state_shape] * CHIPS,
            [pltpu.VMEM((CHIPS, count, DH, DH), BF16)],
            name="spread",
        )
        starts = [swap(spread[n], 2 * n) if n else spread[0] for n in range(CHIPS)]
        states_shape = jax.ShapeDtypeStruct((CHIPS, count, DH, DH), BF16)
        keep, send = local_call(
            functools.partial(enter_kernel, keys),
            [turn if keys == BANDS[0] else lax.optimization_barrier((turn, gates))[0], first, *starts],
            [states_shape, states_shape],
            name="enter",
        )
        for own, state in enumerate((swap(send, 1), keep)):
            finals[own] += [state, *queries[own]]
    done = finish(place, gates, finals[1])
    return finish_last(place, gates, done, finals[0])


def solution(mesh):
    spec = P(("groups", "seq"), None)
    return jax.shard_map(
        local,
        mesh=mesh,
        in_specs=(spec, P(), spec, spec, spec, P()),
        out_specs=spec,
        check_vma=False,
    )
```

```python
import functools

import jax
import jax.numpy as jnp
import ml_dtypes
import numpy as np
from jax import lax
from jax.experimental import pallas as pl
from jax.experimental.pallas import tpu as pltpu
from jax.sharding import PartitionSpec as P

KH = 16
VH = 32
DH = 128
CH = 128
CHIPS = 4
PIECE = 4
BANDS = ((0,), (1,))
WIDE = 2 * DH

F32 = jnp.float32
BF16 = jnp.bfloat16


def dot(a, b):
    return jnp.dot(a, b, preferred_element_type=F32)


def halves(x):
    high = x.astype(BF16)
    return high, (x - high.astype(F32)).astype(BF16)


def decay_rows(decays):
    high, low = halves(decays)
    return jnp.concatenate([high, low], axis=0)


def rows_of(keys):
    return 2 * len(keys) * DH + 16


def decays_of(rows):
    rows = rows.astype(F32)
    return rows[:8] + rows[8:]


def head_slice(h):
    return slice(h * DH, (h + 1) * DH)


def rows_kernel(decay_ref, logit_ref, rows_ref):
    s_at = lax.broadcasted_iota(jnp.int32, (CH, CH), 0)
    t_at = lax.broadcasted_iota(jnp.int32, (CH, CH), 1)
    cumulative = jnp.dot(
        decay_ref[...],
        (s_at <= t_at).astype(F32),
        precision=lax.Precision.HIGHEST,
        preferred_element_type=F32,
    )
    beta = 1.0 / (1.0 + jnp.exp(-logit_ref[...].astype(F32)))
    for g in range(VH // PIECE):
        rows_ref[g, :PIECE] = cumulative[g * PIECE : (g + 1) * PIECE]
        rows_ref[g, PIECE:] = beta[g * PIECE : (g + 1) * PIECE]


def taps(padded, w, height):
    total = padded(0) * w[0:1]
    for tap in range(1, 4):
        total = total + padded(tap) * w[tap : tap + 1]
    return (total / (1.0 + jnp.exp(-total))).astype(BF16)


def load_kernel(x_ref, w_ref, x_out, w_out, rim_out, sems):
    copies = [
        pltpu.make_async_copy(x_ref.at[CH - 4 :], rim_out, sems.at[0]),
        pltpu.make_async_copy(w_ref, w_out, sems.at[1]),
    ]
    step = CH // 4
    for i in range(4):
        part = pl.ds(i * step, step)
        copies.append(pltpu.make_async_copy(x_ref.at[part], x_out.at[part], sems.at[2 + i]))
    for copy in copies:
        copy.start()
    for copy in copies:
        copy.wait()


def load(mixed_qkv, conv_weight):
    vmem = pl.BlockSpec(memory_space=pltpu.VMEM)
    return pl.pallas_call(
        load_kernel,
        out_shape=[
            jax.ShapeDtypeStruct(mixed_qkv.shape, BF16),
            jax.ShapeDtypeStruct(conv_weight.shape, BF16),
            jax.ShapeDtypeStruct((4, mixed_qkv.shape[1]), BF16),
        ],
        in_specs=[pl.BlockSpec(memory_space=pl.ANY)] * 2,
        out_specs=[vmem] * 3,
        scratch_shapes=[pltpu.SemaphoreType.DMA((6,))],
        cost_estimate=pl.CostEstimate(flops=100, bytes_accessed=100, transcendentals=0),
        compiler_params=pltpu.CompilerParams(vmem_limit_bytes=4 << 20),
        name="load",
    )(*(pltpu.with_memory_space_constraint(a, pltpu.HBM) for a in (mixed_qkv, conv_weight)))


def conv_kernel(sc_ref, x_ref, w_ref, out_ref, scr):
    owner = 1 - sc_ref[0]
    width = scr.shape[2]
    keys, values = KH // 2 * DH // width, VH // 2 * DH // width
    starts = [KH * DH + (owner * keys + i) * width for i in range(keys)]
    starts += [2 * KH * DH + (owner * values + i) * width for i in range(values)]
    for i, start in enumerate(starts):
        cols = pl.ds(pl.multiple_of(start, width), width)
        scr[i % 2] = x_ref[:, cols].astype(F32)
        w = w_ref[:, cols].astype(F32)
        out_ref[8:, cols] = taps(lambda tap: scr[i % 2, 5 + tap : 5 + tap + CH - 8, :], w, CH - 8)


def early_conv(place, x, conv_weight):
    return local_call(
        conv_kernel,
        [place, x, conv_weight],
        [jax.ShapeDtypeStruct(x.shape, BF16)],
        [pltpu.VMEM((2, CH, 512), F32)],
        flops=10_000_000,
        vmem_mib=4,
        name="conv",
    )[0]


def convolved(x_ref, rim_ref, w_ref, scr, slot, column, width, conv_ref=None):
    cols = pl.ds(pl.multiple_of(column, DH), width)
    w = w_ref[:, cols].astype(F32)
    scr[slot, 4:8, :width] = rim_ref[:, cols].astype(F32)
    if conv_ref is None:
        scr[slot, 8 : 8 + CH, :width] = x_ref[:, cols].astype(F32)
        return taps(lambda tap: scr[slot, 5 + tap : 5 + tap + CH, :width], w, CH).astype(F32)
    scr[slot, 8:16, :width] = x_ref[:8, cols].astype(F32)
    first = taps(lambda tap: scr[slot, 5 + tap : 13 + tap, :width], w, 8)
    rest = conv_ref[:, cols].astype(F32)
    return jnp.concatenate([first.astype(F32), rest[8:]], axis=0)


def inverse_norms(rows, axis):
    return lax.rsqrt(jnp.sum(rows * rows, axis=axis, keepdims=True) + 1e-06)


def decay_pairs(rows, cols, h):
    return jnp.exp(jnp.minimum(cols[:, h : h + 1] - rows[h : h + 1], 0.0))


def token_order():
    t_at = lax.broadcasted_iota(jnp.int32, (CH, CH), 0)
    s_at = lax.broadcasted_iota(jnp.int32, (CH, CH), 1)
    return t_at, s_at


def terms_kernel(keys, sc_ref, x_ref, rim_ref, w_ref, conv_ref, rows_ref, masks_ref, *refs):
    theirs_refs, mine_refs, scr = refs[:3], refs[3:6], refs[6]
    t_at, s_at = token_order()
    strict = t_at > s_at
    unit = (t_at == s_at).astype(F32).astype(BF16)
    pieces = VH // 2 // PIECE
    kd, vd = len(keys) * DH, 2 * len(keys) * DH

    heads = []
    slot = 0
    for own, (ma_ref, solved_ref, key_ref) in enumerate((theirs_refs, mine_refs)):
        owner = sc_ref[0] if own else 1 - sc_ref[0]
        conv = functools.partial(
            convolved, x_ref, rim_ref, w_ref, scr, conv_ref=None if own else conv_ref
        )
        for offset in range(CHIPS):
            piece = owner * pieces + (sc_ref[1] ^ offset)
            key_at = piece * PIECE // 2 + keys[0]
            ck = conv(slot, (KH + key_at) * DH, kd)
            cv = conv(slot + 1, 2 * (KH + key_at) * DH, vd)
            slot += 2
            rows = rows_ref[piece]
            following = pltpu.roll(rows, CH - 1, axis=1)
            cols = rows.T
            grow_cols = jnp.exp(cols)
            tail_rows = jnp.exp(rows[:, CH - 1 : CH] - rows)
            ma_ref[offset, 2 * kd :, :] = decay_rows(
                jnp.broadcast_to(jnp.exp(rows[:, CH - 1 : CH]), (8, WIDE))
            )
            for g, key in enumerate(keys):
                k_f = ck[:, head_slice(g)]
                k_b = k_f.astype(BF16)
                key_ref[offset, g] = k_b
                k_t = k_f.T
                rk_col, rk_row = inverse_norms(k_f, 1), inverse_norms(k_t, 0)
                key_dot = dot(k_b, k_t.astype(BF16)) * rk_col * rk_row
                for i in range(2):
                    h = 2 * key + i
                    system = key_dot * decay_pairs(rows, cols, h)
                    system = jnp.where(strict, system, 0.0).astype(BF16)
                    beta_row = rows[4 + h : 5 + h]
                    gains = jnp.broadcast_to(beta_row * following[4 + h : 5 + h], (CH, CH)).astype(BF16)
                    high, low = halves(jnp.broadcast_to(beta_row, (CH, CH)))
                    heads.append(
                        dict(
                            out=(ma_ref, solved_ref, offset, 2 * g + i),
                            system=system,
                            inv=unit * high - system * masks_ref[0] * gains,
                            inv_low=unit * low,
                            value=cv[:, head_slice(2 * g + i)].astype(BF16),
                            key=(k_f * (grow_cols[:, h : h + 1] * rk_col)).astype(BF16),
                            tail=(k_t * (rk_row * tail_rows[h : h + 1])).astype(BF16),
                        )
                    )

    for level in range(1, 7):
        mask = masks_ref[level]
        steps = [dot(p["inv"], p["system"] * mask).astype(BF16) for p in heads]
        steps = [dot(s, p["inv"]).astype(BF16) for s, p in zip(steps, heads)]
        for s, p in zip(steps, heads):
            p["inv"] = p["inv"] - s

    for p in heads:
        right = jnp.concatenate([p["key"], p["value"]], axis=1)
        p["solved"] = dot(
            jnp.concatenate([p["inv"], p["inv_low"]], axis=1),
            jnp.concatenate([right, right], axis=0),
        ).astype(BF16)
    for p in heads:
        ma_ref, solved_ref, offset, h = p["out"]
        solved = p["solved"]
        solved_ref[offset, h] = solved
        ma_ref[offset, head_slice(h), :] = dot(p["tail"], solved).astype(BF16)


def local_call(
    kernel, args, out_shape, scratch=(), flops=100_000_000, vmem_mib=12, scalars=1, name=None
):
    vmem = pl.BlockSpec(memory_space=pltpu.VMEM)
    in_specs = [pl.BlockSpec(memory_space=pltpu.SMEM)] * scalars + [vmem] * (len(args) - scalars)
    return pl.pallas_call(
        kernel,
        out_shape=out_shape,
        in_specs=in_specs,
        out_specs=[vmem] * len(out_shape),
        scratch_shapes=list(scratch),
        cost_estimate=pl.CostEstimate(flops=100, bytes_accessed=100, transcendentals=0),
        compiler_params=pltpu.CompilerParams(vmem_limit_bytes=vmem_mib << 20),
        name=name,
    )(*args)


def block_terms(keys, place, shared):
    outs = [
        jax.ShapeDtypeStruct((CHIPS, rows_of(keys), WIDE), BF16),
        jax.ShapeDtypeStruct((CHIPS, 2 * len(keys), CH, WIDE), BF16),
        jax.ShapeDtypeStruct((CHIPS, len(keys), CH, DH), BF16),
    ] * 2
    out = local_call(
        functools.partial(terms_kernel, keys),
        [place, *shared],
        outs,
        [pltpu.VMEM((4 * CHIPS, CH + 8, 2 * len(keys) * DH), F32)],
        vmem_mib=40,
        name="terms",
    )
    return out[:3], out[3:]


def compose_kernel(keys, sc_ref, mine_ref, other_ref, first_ref, *sent_refs):
    count = 2 * len(keys)
    is_first = sc_ref[0] == 0
    for offset in range(CHIPS):
        mine_g, theirs_g = decays_at(mine_ref, offset), decays_at(other_ref, offset)
        first_g = jnp.where(is_first, mine_g, theirs_g)
        second_g = jnp.where(is_first, theirs_g, mine_g)
        first_ref[offset, count * DH :, :] = decay_rows(first_g)
        sent_refs[offset][count * DH :, :] = decay_rows(first_g * second_g)
        for h in range(count):
            mine, theirs = mine_ref[offset, head_slice(h)], other_ref[offset, head_slice(h)]
            first = jnp.where(is_first, mine, theirs)
            second = jnp.where(is_first, theirs, mine)
            first_ref[offset, head_slice(h), :] = first
            product = dot(second[:, :DH], first)
            at = 2 * keys[0] + h
            kept = jnp.concatenate(
                [second[:, :DH].astype(F32) * first_g[at : at + 1, :DH], second[:, DH:].astype(F32)],
                axis=1,
            )
            sent_refs[offset][head_slice(h), :] = (
                first.astype(F32) * second_g[at : at + 1] - product + kept
            ).astype(BF16)


def compose(keys, place, mine, other):
    one = jax.ShapeDtypeStruct((rows_of(keys), WIDE), BF16)
    first, *sent = local_call(
        functools.partial(compose_kernel, keys),
        [place, mine, other],
        [jax.ShapeDtypeStruct(mine.shape, BF16)] + [one] * CHIPS,
        vmem_mib=16,
        name="compose",
    )
    return first, sent


def queries_kernel(keys, sc_ref, x_ref, rim_ref, w_ref, rows_ref, *refs):
    ins, outs, scr = (refs[0:2], refs[2:4]), (refs[4:6], refs[6:8]), refs[8]
    t_at, s_at = token_order()
    heads = []
    for own, ((solved_ref, key_ref), out) in enumerate(zip(ins, outs)):
        owner = sc_ref[0] if own else 1 - sc_ref[0]
        for offset in range(CHIPS):
            piece = owner * (VH // 2 // PIECE) + (sc_ref[1] ^ offset)
            kd = len(keys) * DH
            key_at = piece * PIECE // 2 + keys[0]
            cq = convolved(x_ref, rim_ref, w_ref, scr, own * CHIPS + offset, key_at * DH, kd)
            rows = rows_ref[piece]
            cols = rows.T
            grow_cols = jnp.exp(cols)
            for g, key in enumerate(keys):
                q_f = cq[:, head_slice(g)]
                k_t = key_ref[offset, g].astype(F32).T
                rq_col = inverse_norms(q_f, 1) * DH ** (-0.5)
                query_dot = dot(q_f.astype(BF16), k_t.astype(BF16)) * rq_col * inverse_norms(k_t, 0)
                for i in range(2):
                    h = 2 * key + i
                    mixing = query_dot * decay_pairs(rows, cols, h)
                    mixing = halves(jnp.where(t_at >= s_at, mixing, 0.0))
                    query = q_f * (grow_cols[:, h : h + 1] * rq_col)
                    heads.append((solved_ref, out, offset, 2 * g + i, mixing, query))
    for solved_ref, (loc_ref, car_ref), offset, h, mixing, query in heads:
        solved = solved_ref[offset, h]
        both = dot(jnp.concatenate(mixing, axis=1), jnp.concatenate([solved, solved], axis=0))
        loc_ref[offset, h] = both[:, DH:]
        car_ref[offset, h] = (query - both[:, :DH]).astype(BF16)


def block_queries(keys, place, shared, theirs, mine):
    count = 2 * len(keys)
    out = local_call(
        functools.partial(queries_kernel, keys),
        [place, *shared[:3], shared[4], *theirs, *mine],
        [
            jax.ShapeDtypeStruct((CHIPS, count, CH, DH), F32),
            jax.ShapeDtypeStruct((CHIPS, count, CH, DH), BF16),
        ]
        * 2,
        [pltpu.VMEM((2 * CHIPS, CH + 8, len(keys) * DH), F32)],
        vmem_mib=24,
        name="queries",
    )
    return out[:2], out[2:]


def decays_at(ref, slot):
    return decays_of(ref[slot, ref.shape[1] - 16 :])


def advance(keys, ref, slot, h, decays, state):
    mats = ref[slot, head_slice(h)]
    at = 2 * keys[0] + h
    moved = state.astype(F32) * decays[at : at + 1, :DH] - dot(mats[:, :DH], state)
    return (moved + mats[:, DH:].astype(F32)).astype(BF16)


def gather_kernel(keys, sc_ref, p0, p1, p2, p3, in_ref, order_ref, out_ref):
    for offset, piece in enumerate((p0, p1, p2, p3)):
        order_ref[sc_ref[1] ^ offset] = piece[...]

    @pl.when(sc_ref[2] == 0)
    def _():
        states = [in_ref[h] for h in range(2 * len(keys))]
        for chip in range(CHIPS):
            decays = decays_at(order_ref, chip)
            states = [advance(keys, order_ref, chip, h, decays, s) for h, s in enumerate(states)]
        for h, state in enumerate(states):
            out_ref[h] = state

    @pl.when(sc_ref[2] == 1)
    def _():
        out_ref[...] = jnp.zeros_like(out_ref)


def spread_kernel(keys, sc_ref, order_ref, in_ref, o0, o1, o2, o3, scr):
    keep = (1 - sc_ref[3]).astype(BF16)
    states = [in_ref[h] * keep for h in range(2 * len(keys))]
    for chip in range(CHIPS):
        for h, state in enumerate(states):
            scr[chip, h] = state
        if chip < CHIPS - 1:
            decays = decays_at(order_ref, chip)
            states = [advance(keys, order_ref, chip, h, decays, s) for h, s in enumerate(states)]
    for offset, out in enumerate((o0, o1, o2, o3)):
        out[...] = scr[sc_ref[1] ^ offset]


def enter_kernel(keys, sc_ref, first_ref, *refs):
    starts, (keep_ref, send_ref) = refs[:CHIPS], refs[CHIPS:]
    is_first = sc_ref[0] == 0
    for offset in range(CHIPS):
        decays = decays_at(first_ref, offset)
        for h in range(2 * len(keys)):
            start = starts[offset][h]
            after = advance(keys, first_ref, offset, h, decays, start)
            keep_ref[offset, h] = jnp.where(is_first, start, after)
            send_ref[offset, h] = jnp.where(is_first, after, start)


def gates_kernel(gate_ref, gain_ref, out_ref):
    gates = gate_ref[...].astype(F32)
    gates = gates / (1.0 + jnp.exp(-gates))
    for h in range(VH):
        out_ref[:, head_slice(h)] = gates[:, head_slice(h)] * gain_ref[...]


def piece_columns(keys, own, sc_ref, offset):
    owner = sc_ref[0] if own else 1 - sc_ref[0]
    piece = owner * (VH // 2 // PIECE) + (sc_ref[1] ^ offset)
    start = (piece * PIECE + 2 * keys[0]) * DH
    return pl.ds(pl.multiple_of(start, 2 * DH), 2 * len(keys) * DH)


def finish_piece(keys, own, offset, sc_ref, gate_ref, state_ref, loc_ref, car_ref, out_ref):
    gates = gate_ref[:, piece_columns(keys, own, sc_ref, offset)]
    for h in range(2 * len(keys)):
        core = loc_ref[offset, h] + dot(car_ref[offset, h], state_ref[offset, h])
        mean_sq = jnp.mean(core * core, axis=1, keepdims=True)
        cols = head_slice(h)
        scaled = core * lax.rsqrt(mean_sq + 1e-06) * gates[:, cols]
        out_ref[offset, :, cols] = scaled.astype(BF16)


def finish_kernel(parts, sc_ref, gate_ref, *refs):
    for n, (keys, own) in enumerate(parts):
        for offset in range(CHIPS):
            ins = refs[3 * n : 3 * n + 3]
            finish_piece(keys, own, offset, sc_ref, gate_ref, *ins, refs[3 * len(parts) + n])


def finish(parts, place, gates, terms):
    return local_call(
        functools.partial(finish_kernel, parts),
        [place, gates, *sum(terms, [])],
        [jax.ShapeDtypeStruct((CHIPS, CH, 2 * len(keys) * DH), BF16) for keys, _ in parts],
        vmem_mib=4,
        name="finish",
    )


def last_kernel(earlier, keys, own, sc_ref, gate_ref, state_ref, loc_ref, car_ref, *refs):
    done_refs, (out_ref, scr, sems) = refs[: len(earlier)], refs[len(earlier) :]
    copies = []

    def send(source, cols):
        copies.append(pltpu.make_async_copy(source, out_ref.at[:, cols], sems.at[len(copies)]))
        copies[-1].start()

    for part, done_ref in zip(earlier, done_refs):
        for offset in range(CHIPS):
            send(done_ref.at[offset], piece_columns(*part, sc_ref, offset))
    for offset in range(CHIPS):
        finish_piece(keys, own, offset, sc_ref, gate_ref, state_ref, loc_ref, car_ref, scr)
        send(scr.at[offset], piece_columns(keys, own, sc_ref, offset))
    for copy in copies:
        copy.wait()


def finish_last(earlier, part, place, gates, done, terms):
    keys, own = part
    vmem = pl.BlockSpec(memory_space=pltpu.VMEM)
    args = [place, gates, *terms, *done]
    return pl.pallas_call(
        functools.partial(last_kernel, earlier, keys, own),
        out_shape=jax.ShapeDtypeStruct(gates.shape, BF16),
        in_specs=[pl.BlockSpec(memory_space=pltpu.SMEM)] + [vmem] * (len(args) - 1),
        out_specs=pl.BlockSpec(memory_space=pl.ANY),
        scratch_shapes=[
            pltpu.VMEM((CHIPS, CH, 2 * len(keys) * DH), BF16),
            pltpu.SemaphoreType.DMA((CHIPS * (len(earlier) + 1),)),
        ],
        cost_estimate=pl.CostEstimate(flops=100, bytes_accessed=100, transcendentals=0),
        compiler_params=pltpu.CompilerParams(vmem_limit_bytes=4 << 20),
        name="finish_last",
    )(*args)


def shift(block, distance):
    count = lax.axis_size("seq")
    return lax.ppermute(block, "seq", [(i, i + distance) for i in range(count - distance)])


def swap(block, distance):
    return lax.ppermute(block, "seq", [(i, i ^ distance) for i in range(lax.axis_size("seq"))])


def level_masks():
    t_at, s_at = np.arange(CH)[:, None], np.arange(CH)[None, :]
    return np.stack(
        [(t_at > s_at) & ((t_at ^ s_at) >> level == 1) for level in range(7)]
    ).astype(ml_dtypes.bfloat16)


def local(mixed_qkv, conv_weight, beta_logit, log_decay, gate_in, norm_gain):
    at = lax.axis_index("seq")
    last = at // (2 * CHIPS) == lax.axis_size("seq") // (2 * CHIPS) - 1
    place = jnp.stack([at % 2, (at // 2) % CHIPS, last.astype(at.dtype), (at < 2 * CHIPS).astype(at.dtype)])
    x, weight, last_rows = load(mixed_qkv, conv_weight)
    rim = shift(last_rows, 1)
    (rows,) = local_call(
        rows_kernel,
        [log_decay.T, beta_logit.T],
        [jax.ShapeDtypeStruct((VH // PIECE, 2 * PIECE, CH), F32)],
        scalars=0,
        name="rows",
    )
    conv_out = early_conv(place, x, weight)
    shared = (x, rim, weight, conv_out, rows, jnp.asarray(level_masks()))
    chips = range(CHIPS)
    hop = swap if lax.axis_size("seq") == 4 * CHIPS else shift
    parts, terms, done = [], [], []
    (gates,) = local_call(
        gates_kernel,
        [gate_in, norm_gain[None]],
        [jax.ShapeDtypeStruct(gate_in.shape, F32)],
        scalars=0,
        vmem_mib=4,
        name="gates",
    )
    for keys in BANDS:
        theirs, mine = block_terms(keys, place, shared)
        other = swap(theirs[0], 1)
        first, sent = compose(keys, place, mine[0], other)
        pieces = [swap(sent[n], 2 * n) if n else sent[0] for n in range(CHIPS)]
        queries = block_queries(keys, place, shared, theirs[1:], mine[1:])
        turn, _ = lax.optimization_barrier((place, queries))

        count = 2 * len(keys)
        state_shape = jax.ShapeDtypeStruct((count, DH, DH), BF16)
        order_shape = jax.ShapeDtypeStruct((CHIPS, rows_of(keys), WIDE), BF16)
        entering = jnp.zeros((count, DH, DH), BF16)
        for _ in range(max(lax.axis_size("seq") // (2 * CHIPS) - 1, 1)):
            order, leaving = local_call(
                functools.partial(gather_kernel, keys),
                [turn, *pieces, entering],
                [order_shape, state_shape],
                name="gather",
            )
            entering = hop(leaving, 2 * CHIPS)
        spread = local_call(
            functools.partial(spread_kernel, keys),
            [place, order, entering],
            [state_shape] * CHIPS,
            [pltpu.VMEM((CHIPS, count, DH, DH), BF16)],
            name="spread",
        )
        starts = [swap(spread[n], 2 * n) if n else spread[0] for n in range(CHIPS)]
        states_shape = jax.ShapeDtypeStruct((CHIPS, count, DH, DH), BF16)
        keep, send = local_call(
            functools.partial(enter_kernel, keys),
            [turn if keys == BANDS[0] else lax.optimization_barrier((turn, gates))[0], first, *starts],
            [states_shape, states_shape],
            name="enter",
        )
        for own, state in ((1, keep), (0, swap(send, 1))):
            parts.append((keys, own))
            terms.append([state, *queries[own]])
    done = finish(parts[:-1], place, gates, terms[:-1])
    return finish_last(parts[:-1], parts[-1], place, gates, done, terms[-1])


def solution(mesh):
    spec = P(("groups", "seq"), None)
    return jax.shard_map(
        local,
        mesh=mesh,
        in_specs=(spec, P(), spec, spec, spec, P()),
        out_specs=spec,
        check_vma=False,
    )
```

```python
import functools

import jax
import jax.numpy as jnp
import ml_dtypes
import numpy as np
from jax import lax
from jax.experimental import pallas as pl
from jax.experimental.pallas import tpu as pltpu
from jax.sharding import PartitionSpec as P

KH = 16
VH = 32
DH = 128
CH = 128
CHIPS = 4
PIECE = 4
BANDS = ((0,), (1,))
WIDE = 2 * DH

F32 = jnp.float32
BF16 = jnp.bfloat16


def dot(a, b):
    return jnp.dot(a, b, preferred_element_type=F32)


def halves(x):
    high = x.astype(BF16)
    return high, (x - high.astype(F32)).astype(BF16)


def decay_rows(decays):
    decays = decays[:PIECE]
    high = decays.astype(BF16).astype(F32)
    return jnp.concatenate([high, decays - high], axis=0).astype(BF16)


def rows_of(keys):
    return 2 * len(keys) * DH + 2 * PIECE


def decays_of(rows):
    rows = rows.astype(F32)
    return rows[:PIECE] + rows[PIECE:]


def head_slice(h):
    return slice(h * DH, (h + 1) * DH)


def rows_kernel(decay_ref, logit_ref, rows_ref):
    s_at = lax.broadcasted_iota(jnp.int32, (CH, CH), 0)
    t_at = lax.broadcasted_iota(jnp.int32, (CH, CH), 1)
    cumulative = jnp.dot(
        decay_ref[...],
        (s_at <= t_at).astype(F32),
        precision=lax.Precision.HIGHEST,
        preferred_element_type=F32,
    )
    beta = 1.0 / (1.0 + jnp.exp(-logit_ref[...].astype(F32)))
    for g in range(VH // PIECE):
        rows_ref[g, :PIECE] = cumulative[g * PIECE : (g + 1) * PIECE]
        rows_ref[g, PIECE:] = beta[g * PIECE : (g + 1) * PIECE]


def taps(padded, w, height):
    total = padded(0) * w[0:1]
    for tap in range(1, 4):
        total = total + padded(tap) * w[tap : tap + 1]
    return (total / (1.0 + jnp.exp(-total))).astype(BF16)


def load_kernel(x_ref, w_ref, x_out, w_out, rim_out, sems):
    copies = [
        pltpu.make_async_copy(x_ref.at[CH - 4 :], rim_out, sems.at[0]),
        pltpu.make_async_copy(w_ref, w_out, sems.at[1]),
    ]
    step = CH // 4
    for i in range(4):
        part = pl.ds(i * step, step)
        copies.append(pltpu.make_async_copy(x_ref.at[part], x_out.at[part], sems.at[2 + i]))
    for copy in copies:
        copy.start()
    for copy in copies:
        copy.wait()


def load(mixed_qkv, conv_weight):
    vmem = pl.BlockSpec(memory_space=pltpu.VMEM)
    return pl.pallas_call(
        load_kernel,
        out_shape=[
            jax.ShapeDtypeStruct(mixed_qkv.shape, BF16),
            jax.ShapeDtypeStruct(conv_weight.shape, BF16),
            jax.ShapeDtypeStruct((4, mixed_qkv.shape[1]), BF16),
        ],
        in_specs=[pl.BlockSpec(memory_space=pl.ANY)] * 2,
        out_specs=[vmem] * 3,
        scratch_shapes=[pltpu.SemaphoreType.DMA((6,))],
        cost_estimate=pl.CostEstimate(flops=100, bytes_accessed=100, transcendentals=0),
        compiler_params=pltpu.CompilerParams(vmem_limit_bytes=4 << 20),
        name="load",
    )(*(pltpu.with_memory_space_constraint(a, pltpu.HBM) for a in (mixed_qkv, conv_weight)))


def conv_kernel(sc_ref, x_ref, w_ref, decay_ref, logit_ref, out_ref, rows_ref, scr):
    rows_kernel(decay_ref, logit_ref, rows_ref)
    owner = 1 - sc_ref[0]
    width = scr.shape[2]
    keys, values = KH // 2 * DH // width, VH // 2 * DH // width
    starts = [KH * DH + (owner * keys + i) * width for i in range(keys)]
    starts += [2 * KH * DH + (owner * values + i) * width for i in range(values)]
    for i, start in enumerate(starts):
        cols = pl.ds(pl.multiple_of(start, width), width)
        scr[i % 2] = x_ref[:, cols].astype(F32)
        w = w_ref[:, cols].astype(F32)
        out_ref[8:, cols] = taps(lambda tap: scr[i % 2, 5 + tap : 5 + tap + CH - 8, :], w, CH - 8)


def early_conv(place, x, conv_weight, log_decay, beta_logit):
    return local_call(
        conv_kernel,
        [place, x, conv_weight, log_decay.T, beta_logit.T],
        [
            jax.ShapeDtypeStruct(x.shape, BF16),
            jax.ShapeDtypeStruct((VH // PIECE, 2 * PIECE, CH), F32),
        ],
        [pltpu.VMEM((2, CH, 512), F32)],
        vmem_mib=4,
        name="conv",
    )


def convolved(x_ref, rim_ref, w_ref, scr, slot, column, width, conv_ref=None):
    cols = pl.ds(pl.multiple_of(column, DH), width)
    w = w_ref[:, cols].astype(F32)
    scr[slot, 4:8, :width] = rim_ref[:, cols].astype(F32)
    if conv_ref is None:
        scr[slot, 8 : 8 + CH, :width] = x_ref[:, cols].astype(F32)
        return taps(lambda tap: scr[slot, 5 + tap : 5 + tap + CH, :width], w, CH).astype(F32)
    scr[slot, 8:16, :width] = x_ref[:8, cols].astype(F32)
    first = taps(lambda tap: scr[slot, 5 + tap : 13 + tap, :width], w, 8)
    rest = conv_ref[:, cols].astype(F32)
    return jnp.concatenate([first.astype(F32), rest[8:]], axis=0)


def inverse_norms(rows, axis):
    return lax.rsqrt(jnp.sum(rows * rows, axis=axis, keepdims=True) + 1e-06)


def decay_pairs(rows, cols, h):
    return jnp.exp(jnp.minimum(cols[:, h : h + 1] - rows[h : h + 1], 0.0))


def token_order():
    t_at = lax.broadcasted_iota(jnp.int32, (CH, CH), 0)
    s_at = lax.broadcasted_iota(jnp.int32, (CH, CH), 1)
    return t_at, s_at


def terms_kernel(keys, sc_ref, x_ref, rim_ref, w_ref, conv_ref, rows_ref, masks_ref, *refs):
    theirs_refs, mine_refs, scr = refs[:3], refs[3:6], refs[6]
    t_at, s_at = token_order()
    strict = t_at > s_at
    unit = (t_at == s_at).astype(F32).astype(BF16)
    pieces = VH // 2 // PIECE
    kd, vd = len(keys) * DH, 2 * len(keys) * DH

    heads = []
    slot = 0
    for own, (ma_ref, solved_ref, key_ref) in enumerate((theirs_refs, mine_refs)):
        owner = sc_ref[0] if own else 1 - sc_ref[0]
        conv = functools.partial(
            convolved, x_ref, rim_ref, w_ref, scr, conv_ref=None if own else conv_ref
        )
        for offset in range(CHIPS):
            piece = owner * pieces + (sc_ref[1] ^ offset)
            key_at = piece * PIECE // 2 + keys[0]
            ck = conv(slot, (KH + key_at) * DH, kd)
            cv = conv(slot + 1, 2 * (KH + key_at) * DH, vd)
            slot += 2
            rows = rows_ref[piece]
            following = pltpu.roll(rows, CH - 1, axis=1)
            cols = rows.T
            grow_cols = jnp.exp(cols)
            tail_rows = jnp.exp(rows[:, CH - 1 : CH] - rows)
            ma_ref[offset, 2 * kd :, :] = decay_rows(
                jnp.broadcast_to(jnp.exp(rows[:, CH - 1 : CH]), (8, WIDE))
            )
            for g, key in enumerate(keys):
                k_f = ck[:, head_slice(g)]
                k_b = k_f.astype(BF16)
                key_ref[offset, g] = k_b
                k_t = k_f.T
                rk_col, rk_row = inverse_norms(k_f, 1), inverse_norms(k_t, 0)
                key_dot = dot(k_b, k_t.astype(BF16)) * rk_col * rk_row
                for i in range(2):
                    h = 2 * key + i
                    system = key_dot * decay_pairs(rows, cols, h)
                    system = jnp.where(strict, system, 0.0).astype(BF16)
                    beta_row = rows[4 + h : 5 + h]
                    gains = jnp.broadcast_to(beta_row * following[4 + h : 5 + h], (CH, CH)).astype(BF16)
                    high, low = halves(jnp.broadcast_to(beta_row, (CH, CH)))
                    heads.append(
                        dict(
                            out=(ma_ref, solved_ref, offset, 2 * g + i),
                            system=system,
                            inv=unit * high - system * masks_ref[0] * gains,
                            inv_low=unit * low,
                            value=cv[:, head_slice(2 * g + i)].astype(BF16),
                            key=(k_f * (grow_cols[:, h : h + 1] * rk_col)).astype(BF16),
                            tail=(k_t * (rk_row * tail_rows[h : h + 1])).astype(BF16),
                        )
                    )

    for level in range(1, 7):
        mask = masks_ref[level]
        steps = [dot(p["inv"], p["system"] * mask).astype(BF16) for p in heads]
        steps = [dot(s, p["inv"]).astype(BF16) for s, p in zip(steps, heads)]
        for s, p in zip(steps, heads):
            p["inv"] = p["inv"] - s

    for p in heads:
        right = jnp.concatenate([p["key"], p["value"]], axis=1)
        p["solved"] = dot(
            jnp.concatenate([p["inv"], p["inv_low"]], axis=1),
            jnp.concatenate([right, right], axis=0),
        ).astype(BF16)
    for p in heads:
        ma_ref, solved_ref, offset, h = p["out"]
        solved = p["solved"]
        solved_ref[offset, h] = solved
        ma_ref[offset, head_slice(h), :] = dot(p["tail"], solved).astype(BF16)


def local_call(
    kernel, args, out_shape, scratch=(), flops=100_000_000, vmem_mib=12, scalars=1, name=None
):
    vmem = pl.BlockSpec(memory_space=pltpu.VMEM)
    in_specs = [pl.BlockSpec(memory_space=pltpu.SMEM)] * scalars + [vmem] * (len(args) - scalars)
    return pl.pallas_call(
        kernel,
        out_shape=out_shape,
        in_specs=in_specs,
        out_specs=[vmem] * len(out_shape),
        scratch_shapes=list(scratch),
        cost_estimate=pl.CostEstimate(flops=100, bytes_accessed=100, transcendentals=0),
        compiler_params=pltpu.CompilerParams(vmem_limit_bytes=vmem_mib << 20),
        name=name,
    )(*args)


def block_terms(keys, place, shared):
    outs = [
        jax.ShapeDtypeStruct((CHIPS, rows_of(keys), WIDE), BF16),
        jax.ShapeDtypeStruct((CHIPS, 2 * len(keys), CH, WIDE), BF16),
        jax.ShapeDtypeStruct((CHIPS, len(keys), CH, DH), BF16),
    ] * 2
    out = local_call(
        functools.partial(terms_kernel, keys),
        [place, *shared],
        outs,
        [pltpu.VMEM((4 * CHIPS, CH + 8, 2 * len(keys) * DH), F32)],
        vmem_mib=40,
        name="terms",
    )
    return out[:3], out[3:]


def compose_kernel(keys, sc_ref, mine_ref, other_ref, first_ref, *sent_refs):
    count = 2 * len(keys)

    def join(first_in, second_in):
        for offset in range(CHIPS):
            first_g, second_g = decays_at(first_in, offset), decays_at(second_in, offset)
            first_ref[offset] = first_in[offset]
            sent_refs[offset][count * DH :, :] = decay_rows(first_g * second_g)
            for h in range(count):
                first, second = first_in[offset, head_slice(h)], second_in[offset, head_slice(h)]
                product = dot(second[:, :DH], first)
                at = 2 * keys[0] + h
                decay = first_g[at : at + 1, :DH]
                kept = jnp.concatenate(
                    [second[:, :DH].astype(F32) * decay, second[:, DH:].astype(F32)], axis=1
                )
                sent_refs[offset][head_slice(h), :] = (
                    first.astype(F32) * second_g[at : at + 1] - product + kept
                ).astype(BF16)

    @pl.when(sc_ref[0] == 0)
    def _():
        join(mine_ref, other_ref)

    @pl.when(sc_ref[0] == 1)
    def _():
        join(other_ref, mine_ref)


def compose(keys, place, mine, other):
    one = jax.ShapeDtypeStruct((rows_of(keys), WIDE), BF16)
    first, *sent = local_call(
        functools.partial(compose_kernel, keys),
        [place, mine, other],
        [jax.ShapeDtypeStruct(mine.shape, BF16)] + [one] * CHIPS,
        vmem_mib=16,
        name="compose",
    )
    return first, sent


def queries_kernel(sc_ref, x_ref, rim_ref, w_ref, rows_ref, *refs):
    count = len(BANDS)
    ins, outs, scr = refs[: 4 * count], refs[4 * count : 8 * count], refs[-1]
    t_at, s_at = token_order()
    heads = []
    for n in range(2 * count):
        keys, own = BANDS[n // 2], n % 2
        solved_ref, key_ref = ins[2 * n : 2 * n + 2]
        out = outs[2 * n : 2 * n + 2]
        owner = sc_ref[0] if own else 1 - sc_ref[0]
        for offset in range(CHIPS):
            piece = owner * (VH // 2 // PIECE) + (sc_ref[1] ^ offset)
            kd = len(keys) * DH
            key_at = piece * PIECE // 2 + keys[0]
            cq = convolved(x_ref, rim_ref, w_ref, scr, n * CHIPS + offset, key_at * DH, kd)
            rows = rows_ref[piece]
            cols = rows.T
            grow_cols = jnp.exp(cols)
            for g, key in enumerate(keys):
                q_f = cq[:, head_slice(g)]
                k_t = key_ref[offset, g].astype(F32).T
                rq_col = inverse_norms(q_f, 1) * DH ** (-0.5)
                query_dot = dot(q_f.astype(BF16), k_t.astype(BF16)) * rq_col * inverse_norms(k_t, 0)
                for i in range(2):
                    h = 2 * key + i
                    mixing = query_dot * decay_pairs(rows, cols, h)
                    mixing = halves(jnp.where(t_at >= s_at, mixing, 0.0))
                    query = q_f * (grow_cols[:, h : h + 1] * rq_col)
                    heads.append((solved_ref, out, offset, 2 * g + i, mixing, query))
    for solved_ref, (loc_ref, car_ref), offset, h, mixing, query in heads:
        solved = solved_ref[offset, h]
        both = dot(jnp.concatenate(mixing, axis=1), jnp.concatenate([solved, solved], axis=0))
        loc_ref[offset, h] = both[:, DH:]
        car_ref[offset, h] = (query - both[:, :DH]).astype(BF16)


def block_queries(place, shared, solved):
    outs = []
    for keys in BANDS:
        rows = (CHIPS, 2 * len(keys), CH, DH)
        outs += [jax.ShapeDtypeStruct(rows, F32), jax.ShapeDtypeStruct(rows, BF16)] * 2
    width = max(len(keys) for keys in BANDS) * DH
    out = local_call(
        queries_kernel,
        [place, *shared[:3], shared[4], *solved],
        outs,
        [pltpu.VMEM((2 * len(BANDS) * CHIPS, CH + 8, width), F32)],
        vmem_mib=28,
        name="queries",
    )
    return [(out[4 * b : 4 * b + 2], out[4 * b + 2 : 4 * b + 4]) for b in range(len(BANDS))]


def decays_at(ref, slot):
    return decays_of(ref[slot, ref.shape[1] - 2 * PIECE :])


def advance(keys, ref, slot, h, decays, state):
    mats = ref[slot, head_slice(h)]
    at = 2 * keys[0] + h
    moved = state.astype(F32) * decays[at : at + 1, :DH] - dot(mats[:, :DH], state)
    return (moved + mats[:, DH:].astype(F32)).astype(BF16)


def gather_kernel(keys, sc_ref, p0, p1, p2, p3, in_ref, order_ref, out_ref):
    for offset, piece in enumerate((p0, p1, p2, p3)):
        order_ref[sc_ref[1] ^ offset] = piece[...]

    @pl.when(sc_ref[2] == 0)
    def _():
        states = [in_ref[h] for h in range(2 * len(keys))]
        for chip in range(CHIPS):
            decays = decays_at(order_ref, chip)
            states = [advance(keys, order_ref, chip, h, decays, s) for h, s in enumerate(states)]
        for h, state in enumerate(states):
            out_ref[h] = state

    @pl.when(sc_ref[2] == 1)
    def _():
        out_ref[...] = jnp.zeros_like(out_ref)


def spread_kernel(keys, sc_ref, order_ref, in_ref, o0, o1, o2, o3, scr):
    keep = (1 - sc_ref[3]).astype(BF16)
    states = [in_ref[h] * keep for h in range(2 * len(keys))]
    for chip in range(CHIPS):
        for h, state in enumerate(states):
            scr[chip, h] = state
        if chip < CHIPS - 1:
            decays = decays_at(order_ref, chip)
            states = [advance(keys, order_ref, chip, h, decays, s) for h, s in enumerate(states)]
    for offset, out in enumerate((o0, o1, o2, o3)):
        out[...] = scr[sc_ref[1] ^ offset]


def enter_kernel(keys, sc_ref, first_ref, *refs):
    starts, (keep_ref, send_ref) = refs[:CHIPS], refs[CHIPS:]
    is_first = sc_ref[0] == 0
    for offset in range(CHIPS):
        decays = decays_at(first_ref, offset)
        for h in range(2 * len(keys)):
            start = starts[offset][h]
            after = advance(keys, first_ref, offset, h, decays, start)
            keep_ref[offset, h] = jnp.where(is_first, start, after)
            send_ref[offset, h] = jnp.where(is_first, after, start)


def gates_kernel(gate_ref, gain_ref, out_ref):
    gates = gate_ref[...].astype(F32)
    gates = gates / (1.0 + jnp.exp(-gates))
    for h in range(VH):
        out_ref[:, head_slice(h)] = gates[:, head_slice(h)] * gain_ref[...]


def piece_columns(keys, own, sc_ref, offset):
    owner = sc_ref[0] if own else 1 - sc_ref[0]
    piece = owner * (VH // 2 // PIECE) + (sc_ref[1] ^ offset)
    start = (piece * PIECE + 2 * keys[0]) * DH
    return pl.ds(pl.multiple_of(start, 2 * DH), 2 * len(keys) * DH)


def finish_piece(keys, own, offset, sc_ref, gate_ref, state_ref, loc_ref, car_ref, out_ref):
    gates = gate_ref[:, piece_columns(keys, own, sc_ref, offset)]
    for h in range(2 * len(keys)):
        core = loc_ref[offset, h] + dot(car_ref[offset, h], state_ref[offset, h])
        mean_sq = jnp.mean(core * core, axis=1, keepdims=True)
        cols = head_slice(h)
        scaled = core * lax.rsqrt(mean_sq + 1e-06) * gates[:, cols]
        out_ref[offset, :, cols] = scaled.astype(BF16)


def finish_kernel(parts, sc_ref, gate_ref, *refs):
    for n, (keys, own) in enumerate(parts):
        for offset in range(CHIPS):
            ins = refs[3 * n : 3 * n + 3]
            finish_piece(keys, own, offset, sc_ref, gate_ref, *ins, refs[3 * len(parts) + n])


def finish(parts, place, gates, terms):
    return local_call(
        functools.partial(finish_kernel, parts),
        [place, gates, *sum(terms, [])],
        [jax.ShapeDtypeStruct((CHIPS, CH, 2 * len(keys) * DH), BF16) for keys, _ in parts],
        vmem_mib=4,
        name="finish",
    )


def last_kernel(earlier, keys, own, sc_ref, gate_ref, state_ref, loc_ref, car_ref, *refs):
    done_refs, (out_ref, scr, sems) = refs[: len(earlier)], refs[len(earlier) :]
    copies = []

    def send(source, cols):
        copies.append(pltpu.make_async_copy(source, out_ref.at[:, cols], sems.at[len(copies)]))
        copies[-1].start()

    for part, done_ref in zip(earlier, done_refs):
        for offset in range(CHIPS):
            send(done_ref.at[offset], piece_columns(*part, sc_ref, offset))
    for offset in range(CHIPS):
        finish_piece(keys, own, offset, sc_ref, gate_ref, state_ref, loc_ref, car_ref, scr)
        send(scr.at[offset], piece_columns(keys, own, sc_ref, offset))
    for copy in copies:
        copy.wait()


def finish_last(earlier, part, place, gates, done, terms):
    keys, own = part
    vmem = pl.BlockSpec(memory_space=pltpu.VMEM)
    args = [place, gates, *terms, *done]
    return pl.pallas_call(
        functools.partial(last_kernel, earlier, keys, own),
        out_shape=jax.ShapeDtypeStruct(gates.shape, BF16),
        in_specs=[pl.BlockSpec(memory_space=pltpu.SMEM)] + [vmem] * (len(args) - 1),
        out_specs=pl.BlockSpec(memory_space=pl.ANY),
        scratch_shapes=[
            pltpu.VMEM((CHIPS, CH, 2 * len(keys) * DH), BF16),
            pltpu.SemaphoreType.DMA((CHIPS * (len(earlier) + 1),)),
        ],
        cost_estimate=pl.CostEstimate(flops=100, bytes_accessed=100, transcendentals=0),
        compiler_params=pltpu.CompilerParams(vmem_limit_bytes=4 << 20),
        name="finish_last",
    )(*args)


def shift(block, distance):
    count = lax.axis_size("seq")
    return lax.ppermute(block, "seq", [(i, i + distance) for i in range(count - distance)])


def swap(block, distance):
    return lax.ppermute(block, "seq", [(i, i ^ distance) for i in range(lax.axis_size("seq"))])


def level_masks():
    t_at, s_at = np.arange(CH)[:, None], np.arange(CH)[None, :]
    return np.stack(
        [(t_at > s_at) & ((t_at ^ s_at) >> level == 1) for level in range(7)]
    ).astype(ml_dtypes.bfloat16)


def local(mixed_qkv, conv_weight, beta_logit, log_decay, gate_in, norm_gain):
    at = lax.axis_index("seq")
    last = at // (2 * CHIPS) == lax.axis_size("seq") // (2 * CHIPS) - 1
    place = jnp.stack([at % 2, (at // 2) % CHIPS, last.astype(at.dtype), (at < 2 * CHIPS).astype(at.dtype)])
    x, weight, last_rows = load(mixed_qkv, conv_weight)
    rim = shift(last_rows, 1)
    conv_out, rows = early_conv(place, x, weight, log_decay, beta_logit)
    shared = (x, rim, weight, conv_out, rows, jnp.asarray(level_masks()))
    chips = range(CHIPS)
    hop = swap if lax.axis_size("seq") == 4 * CHIPS else shift
    parts, terms, done = [], [], []
    (gates,) = local_call(
        gates_kernel,
        [gate_in, norm_gain[None]],
        [jax.ShapeDtypeStruct(gate_in.shape, F32)],
        scalars=0,
        vmem_mib=4,
        name="gates",
    )
    firsts, traveled, solved = [], [], []
    for keys in BANDS:
        theirs, mine = block_terms(keys, place, shared)
        other = swap(theirs[0], 1)
        first, sent = compose(keys, place, mine[0], other)
        firsts.append(first)
        traveled.append([swap(sent[n], 2 * n) if n else sent[0] for n in range(CHIPS)])
        solved += [*theirs[1:], *mine[1:]]
    all_queries = block_queries(place, shared, solved)
    turn, _ = lax.optimization_barrier((place, all_queries))

    for keys, first, pieces, queries in zip(BANDS, firsts, traveled, all_queries):
        count = 2 * len(keys)
        state_shape = jax.ShapeDtypeStruct((count, DH, DH), BF16)
        order_shape = jax.ShapeDtypeStruct((CHIPS, rows_of(keys), WIDE), BF16)
        entering = jnp.zeros((count, DH, DH), BF16)
        for _ in range(max(lax.axis_size("seq") // (2 * CHIPS) - 1, 1)):
            order, leaving = local_call(
                functools.partial(gather_kernel, keys),
                [turn, *pieces, entering],
                [order_shape, state_shape],
                name="gather",
            )
            entering = hop(leaving, 2 * CHIPS)
        spread = local_call(
            functools.partial(spread_kernel, keys),
            [place, order, entering],
            [state_shape] * CHIPS,
            [pltpu.VMEM((CHIPS, count, DH, DH), BF16)],
            name="spread",
        )
        starts = [swap(spread[n], 2 * n) if n else spread[0] for n in range(CHIPS)]
        states_shape = jax.ShapeDtypeStruct((CHIPS, count, DH, DH), BF16)
        keep, send = local_call(
            functools.partial(enter_kernel, keys),
            [turn if keys == BANDS[0] else lax.optimization_barrier((turn, gates))[0], first, *starts],
            [states_shape, states_shape],
            name="enter",
        )
        for own, state in ((1, keep), (0, swap(send, 1))):
            parts.append((keys, own))
            terms.append([state, *queries[own]])
    done = finish(parts[:-1], place, gates, terms[:-1])
    return finish_last(parts[:-1], parts[-1], place, gates, done, terms[-1])


def solution(mesh):
    spec = P(("groups", "seq"), None)
    return jax.shard_map(
        local,
        mesh=mesh,
        in_specs=(spec, P(), spec, spec, spec, P()),
        out_specs=spec,
        check_vma=False,
    )
```

```python
import functools

import jax
import jax.numpy as jnp
import ml_dtypes
import numpy as np
from jax import lax
from jax.experimental import pallas as pl
from jax.experimental.pallas import tpu as pltpu
from jax.sharding import PartitionSpec as P

KH = 16
VH = 32
DH = 128
CH = 128
CHIPS = 4
PIECE = 4
BANDS = ((0,), (1,))
WIDE = 2 * DH

F32 = jnp.float32
BF16 = jnp.bfloat16


def dot(a, b):
    return jnp.dot(a, b, preferred_element_type=F32)


def halves(x):
    high = x.astype(BF16)
    return high, (x - high.astype(F32)).astype(BF16)


def decay_rows(decays):
    decays = decays[:PIECE]
    high = decays.astype(BF16).astype(F32)
    return jnp.concatenate([high, decays - high], axis=0).astype(BF16)


def rows_of(keys):
    return 2 * len(keys) * DH + 2 * PIECE


def decays_of(rows):
    rows = rows.astype(F32)
    return rows[:PIECE] + rows[PIECE:]


def head_slice(h):
    return slice(h * DH, (h + 1) * DH)


def rows_kernel(decay_ref, logit_ref, rows_ref):
    s_at = lax.broadcasted_iota(jnp.int32, (CH, CH), 0)
    t_at = lax.broadcasted_iota(jnp.int32, (CH, CH), 1)
    cumulative = jnp.dot(
        decay_ref[...],
        (s_at <= t_at).astype(F32),
        precision=lax.Precision.HIGHEST,
        preferred_element_type=F32,
    )
    beta = 1.0 / (1.0 + jnp.exp(-logit_ref[...].astype(F32)))
    for g in range(VH // PIECE):
        rows_ref[g, :PIECE] = cumulative[g * PIECE : (g + 1) * PIECE]
        rows_ref[g, PIECE:] = beta[g * PIECE : (g + 1) * PIECE]


def taps(padded, w, height):
    total = padded(0) * w[0:1]
    for tap in range(1, 4):
        total = total + padded(tap) * w[tap : tap + 1]
    return (total / (1.0 + jnp.exp(-total))).astype(BF16)


def load_kernel(x_ref, w_ref, x_out, w_out, rim_out, sems):
    copies = [
        pltpu.make_async_copy(x_ref.at[CH - 4 :], rim_out, sems.at[0]),
        pltpu.make_async_copy(w_ref, w_out, sems.at[1]),
    ]
    step = CH // 4
    for i in range(4):
        part = pl.ds(i * step, step)
        copies.append(pltpu.make_async_copy(x_ref.at[part], x_out.at[part], sems.at[2 + i]))
    for copy in copies:
        copy.start()
    for copy in copies:
        copy.wait()


def load(mixed_qkv, conv_weight):
    vmem = pl.BlockSpec(memory_space=pltpu.VMEM)
    return pl.pallas_call(
        load_kernel,
        out_shape=[
            jax.ShapeDtypeStruct(mixed_qkv.shape, BF16),
            jax.ShapeDtypeStruct(conv_weight.shape, BF16),
            jax.ShapeDtypeStruct((4, mixed_qkv.shape[1]), BF16),
        ],
        in_specs=[pl.BlockSpec(memory_space=pl.ANY)] * 2,
        out_specs=[vmem] * 3,
        scratch_shapes=[pltpu.SemaphoreType.DMA((6,))],
        cost_estimate=pl.CostEstimate(flops=100, bytes_accessed=100, transcendentals=0),
        compiler_params=pltpu.CompilerParams(vmem_limit_bytes=4 << 20),
        name="load",
    )(*(pltpu.with_memory_space_constraint(a, pltpu.HBM) for a in (mixed_qkv, conv_weight)))


def conv_kernel(sc_ref, x_ref, w_ref, decay_ref, logit_ref, out_ref, rows_ref, scr):
    rows_kernel(decay_ref, logit_ref, rows_ref)
    owner = 1 - sc_ref[0]
    width = scr.shape[2]
    keys, values = KH // 2 * DH // width, VH // 2 * DH // width
    starts = [KH * DH + (owner * keys + i) * width for i in range(keys)]
    starts += [2 * KH * DH + (owner * values + i) * width for i in range(values)]
    for i, start in enumerate(starts):
        cols = pl.ds(pl.multiple_of(start, width), width)
        scr[i % 2] = x_ref[:, cols].astype(F32)
        w = w_ref[:, cols].astype(F32)
        out_ref[8:, cols] = taps(lambda tap: scr[i % 2, 5 + tap : 5 + tap + CH - 8, :], w, CH - 8)


def early_conv(place, x, conv_weight, log_decay, beta_logit):
    return local_call(
        conv_kernel,
        [place, x, conv_weight, log_decay.T, beta_logit.T],
        [
            jax.ShapeDtypeStruct(x.shape, BF16),
            jax.ShapeDtypeStruct((VH // PIECE, 2 * PIECE, CH), F32),
        ],
        [pltpu.VMEM((2, CH, 512), F32)],
        vmem_mib=4,
        name="conv",
    )


def convolved(x_ref, rim_ref, w_ref, scr, slot, column, width, conv_ref=None):
    cols = pl.ds(pl.multiple_of(column, DH), width)
    w = w_ref[:, cols].astype(F32)
    scr[slot, 4:8, :width] = rim_ref[:, cols].astype(F32)
    if conv_ref is None:
        scr[slot, 8 : 8 + CH, :width] = x_ref[:, cols].astype(F32)
        return taps(lambda tap: scr[slot, 5 + tap : 5 + tap + CH, :width], w, CH).astype(F32)
    scr[slot, 8:16, :width] = x_ref[:8, cols].astype(F32)
    first = taps(lambda tap: scr[slot, 5 + tap : 13 + tap, :width], w, 8)
    rest = conv_ref[:, cols].astype(F32)
    return jnp.concatenate([first.astype(F32), rest[8:]], axis=0)


def inverse_norms(rows, axis):
    return lax.rsqrt(jnp.sum(rows * rows, axis=axis, keepdims=True) + 1e-06)


def decay_pairs(rows, cols, h):
    return jnp.exp(jnp.minimum(cols[:, h : h + 1] - rows[h : h + 1], 0.0))


def token_order():
    t_at = lax.broadcasted_iota(jnp.int32, (CH, CH), 0)
    s_at = lax.broadcasted_iota(jnp.int32, (CH, CH), 1)
    return t_at, s_at


def terms_kernel(keys, sc_ref, x_ref, rim_ref, w_ref, conv_ref, rows_ref, masks_ref, *refs):
    theirs_refs, mine_refs, scr = refs[:3], refs[3:6], refs[6]
    t_at, s_at = token_order()
    strict = t_at > s_at
    unit = (t_at == s_at).astype(F32).astype(BF16)
    pieces = VH // 2 // PIECE
    kd, vd = len(keys) * DH, 2 * len(keys) * DH

    heads = []
    slot = 0
    for own, (ma_ref, solved_ref, key_ref) in enumerate((theirs_refs, mine_refs)):
        owner = sc_ref[0] if own else 1 - sc_ref[0]
        conv = functools.partial(
            convolved, x_ref, rim_ref, w_ref, scr, conv_ref=None if own else conv_ref
        )
        for offset in range(CHIPS):
            piece = owner * pieces + (sc_ref[1] ^ offset)
            key_at = piece * PIECE // 2 + keys[0]
            ck = conv(slot, (KH + key_at) * DH, kd)
            cv = conv(slot + 1, 2 * (KH + key_at) * DH, vd)
            slot += 2
            rows = rows_ref[piece]
            following = pltpu.roll(rows, CH - 1, axis=1)
            cols = rows.T
            grow_cols = jnp.exp(cols)
            tail_rows = jnp.exp(rows[:, CH - 1 : CH] - rows)
            ma_ref[offset, 2 * kd :, :] = decay_rows(
                jnp.broadcast_to(jnp.exp(rows[:, CH - 1 : CH]), (8, WIDE))
            )
            for g, key in enumerate(keys):
                k_f = ck[:, head_slice(g)]
                k_b = k_f.astype(BF16)
                key_ref[offset, g] = k_b
                k_t = k_f.T
                rk_col, rk_row = inverse_norms(k_f, 1), inverse_norms(k_t, 0)
                key_dot = dot(k_b, k_t.astype(BF16)) * rk_col * rk_row
                for i in range(2):
                    h = 2 * key + i
                    system = key_dot * decay_pairs(rows, cols, h)
                    system = jnp.where(strict, system, 0.0).astype(BF16)
                    beta_row = rows[4 + h : 5 + h]
                    gains = jnp.broadcast_to(beta_row * following[4 + h : 5 + h], (CH, CH)).astype(BF16)
                    high = jnp.broadcast_to(beta_row, (CH, CH)).astype(BF16)
                    heads.append(
                        dict(
                            out=(ma_ref, solved_ref, offset, 2 * g + i),
                            system=system,
                            inv=unit * high - system * masks_ref[0] * gains,
                            value=cv[:, head_slice(2 * g + i)].astype(BF16),
                            key=(k_f * (grow_cols[:, h : h + 1] * rk_col)).astype(BF16),
                            tail=(k_t * (rk_row * tail_rows[h : h + 1])).astype(BF16),
                        )
                    )

    for level in range(1, 7):
        mask = masks_ref[level]
        steps = [dot(p["inv"], p["system"] * mask).astype(BF16) for p in heads]
        steps = [dot(s, p["inv"]).astype(BF16) for s, p in zip(steps, heads)]
        for s, p in zip(steps, heads):
            p["inv"] = p["inv"] - s

    for p in heads:
        right = jnp.concatenate([p["key"], p["value"]], axis=1)
        p["solved"] = dot(
            p["inv"],
            right,
        ).astype(BF16)
    for p in heads:
        ma_ref, solved_ref, offset, h = p["out"]
        solved = p["solved"]
        solved_ref[offset, h] = solved
        ma_ref[offset, head_slice(h), :] = dot(p["tail"], solved).astype(BF16)


def local_call(
    kernel, args, out_shape, scratch=(), flops=100_000_000, vmem_mib=12, scalars=1, name=None
):
    vmem = pl.BlockSpec(memory_space=pltpu.VMEM)
    in_specs = [pl.BlockSpec(memory_space=pltpu.SMEM)] * scalars + [vmem] * (len(args) - scalars)
    return pl.pallas_call(
        kernel,
        out_shape=out_shape,
        in_specs=in_specs,
        out_specs=[vmem] * len(out_shape),
        scratch_shapes=list(scratch),
        cost_estimate=pl.CostEstimate(flops=100, bytes_accessed=100, transcendentals=0),
        compiler_params=pltpu.CompilerParams(vmem_limit_bytes=vmem_mib << 20),
        name=name,
    )(*args)


def block_terms(keys, place, shared):
    outs = [
        jax.ShapeDtypeStruct((CHIPS, rows_of(keys), WIDE), BF16),
        jax.ShapeDtypeStruct((CHIPS, 2 * len(keys), CH, WIDE), BF16),
        jax.ShapeDtypeStruct((CHIPS, len(keys), CH, DH), BF16),
    ] * 2
    out = local_call(
        functools.partial(terms_kernel, keys),
        [place, *shared],
        outs,
        [pltpu.VMEM((4 * CHIPS, CH + 8, 2 * len(keys) * DH), F32)],
        vmem_mib=40,
        name="terms",
    )
    return out[:3], out[3:]


def compose_kernel(keys, sc_ref, mine_ref, other_ref, first_ref, *sent_refs):
    count = 2 * len(keys)

    def join(first_in, second_in):
        for offset in range(CHIPS):
            first_g, second_g = decays_at(first_in, offset), decays_at(second_in, offset)
            first_ref[offset] = first_in[offset]
            sent_refs[offset][count * DH :, :] = decay_rows(first_g * second_g)
            for h in range(count):
                first, second = first_in[offset, head_slice(h)], second_in[offset, head_slice(h)]
                product = dot(second[:, :DH], first)
                at = 2 * keys[0] + h
                decay = first_g[at : at + 1, :DH]
                kept = jnp.concatenate(
                    [second[:, :DH].astype(F32) * decay, second[:, DH:].astype(F32)], axis=1
                )
                sent_refs[offset][head_slice(h), :] = (
                    first.astype(F32) * second_g[at : at + 1] - product + kept
                ).astype(BF16)

    @pl.when(sc_ref[0] == 0)
    def _():
        join(mine_ref, other_ref)

    @pl.when(sc_ref[0] == 1)
    def _():
        join(other_ref, mine_ref)


def compose(keys, place, mine, other):
    one = jax.ShapeDtypeStruct((rows_of(keys), WIDE), BF16)
    first, *sent = local_call(
        functools.partial(compose_kernel, keys),
        [place, mine, other],
        [jax.ShapeDtypeStruct(mine.shape, BF16)] + [one] * CHIPS,
        vmem_mib=16,
        name="compose",
    )
    return first, sent


def queries_kernel(sc_ref, x_ref, rim_ref, w_ref, rows_ref, *refs):
    count = len(BANDS)
    ins, outs, scr = refs[: 4 * count], refs[4 * count : 8 * count], refs[-1]
    t_at, s_at = token_order()
    heads = []
    for n in range(2 * count):
        keys, own = BANDS[n // 2], n % 2
        solved_ref, key_ref = ins[2 * n : 2 * n + 2]
        out = outs[2 * n : 2 * n + 2]
        owner = sc_ref[0] if own else 1 - sc_ref[0]
        for offset in range(CHIPS):
            piece = owner * (VH // 2 // PIECE) + (sc_ref[1] ^ offset)
            kd = len(keys) * DH
            key_at = piece * PIECE // 2 + keys[0]
            cq = convolved(x_ref, rim_ref, w_ref, scr, n * CHIPS + offset, key_at * DH, kd)
            rows = rows_ref[piece]
            cols = rows.T
            grow_cols = jnp.exp(cols)
            for g, key in enumerate(keys):
                q_f = cq[:, head_slice(g)]
                k_t = key_ref[offset, g].astype(F32).T
                rq_col = inverse_norms(q_f, 1) * DH ** (-0.5)
                query_dot = dot(q_f.astype(BF16), k_t.astype(BF16)) * rq_col * inverse_norms(k_t, 0)
                for i in range(2):
                    h = 2 * key + i
                    mixing = query_dot * decay_pairs(rows, cols, h)
                    mixing = halves(jnp.where(t_at >= s_at, mixing, 0.0))
                    query = q_f * (grow_cols[:, h : h + 1] * rq_col)
                    heads.append((solved_ref, out, offset, 2 * g + i, mixing, query))
    for solved_ref, (loc_ref, car_ref), offset, h, mixing, query in heads:
        solved = solved_ref[offset, h]
        both = dot(jnp.concatenate(mixing, axis=1), jnp.concatenate([solved, solved], axis=0))
        loc_ref[offset, h] = both[:, DH:]
        car_ref[offset, h] = (query - both[:, :DH]).astype(BF16)


def block_queries(place, shared, solved):
    outs = []
    for keys in BANDS:
        rows = (CHIPS, 2 * len(keys), CH, DH)
        outs += [jax.ShapeDtypeStruct(rows, F32), jax.ShapeDtypeStruct(rows, BF16)] * 2
    width = max(len(keys) for keys in BANDS) * DH
    out = local_call(
        queries_kernel,
        [place, *shared[:3], shared[4], *solved],
        outs,
        [pltpu.VMEM((2 * len(BANDS) * CHIPS, CH + 8, width), F32)],
        vmem_mib=28,
        name="queries",
    )
    return [(out[4 * b : 4 * b + 2], out[4 * b + 2 : 4 * b + 4]) for b in range(len(BANDS))]


def decays_at(ref, slot):
    return decays_of(ref[slot, ref.shape[1] - 2 * PIECE :])


def advance(keys, ref, slot, h, decays, state):
    mats = ref[slot, head_slice(h)]
    at = 2 * keys[0] + h
    moved = state.astype(F32) * decays[at : at + 1, :DH] - dot(mats[:, :DH], state)
    return (moved + mats[:, DH:].astype(F32)).astype(BF16)


def gather_kernel(keys, sc_ref, p0, p1, p2, p3, in_ref, order_ref, out_ref):
    for offset, piece in enumerate((p0, p1, p2, p3)):
        order_ref[sc_ref[1] ^ offset] = piece[...]

    @pl.when(sc_ref[2] == 0)
    def _():
        states = [in_ref[h] for h in range(2 * len(keys))]
        for chip in range(CHIPS):
            decays = decays_at(order_ref, chip)
            states = [advance(keys, order_ref, chip, h, decays, s) for h, s in enumerate(states)]
        for h, state in enumerate(states):
            out_ref[h] = state

    @pl.when(sc_ref[2] == 1)
    def _():
        out_ref[...] = jnp.zeros_like(out_ref)


def spread_kernel(keys, sc_ref, order_ref, in_ref, o0, o1, o2, o3, scr):
    keep = (1 - sc_ref[3]).astype(BF16)
    states = [in_ref[h] * keep for h in range(2 * len(keys))]
    for chip in range(CHIPS):
        for h, state in enumerate(states):
            scr[chip, h] = state
        if chip < CHIPS - 1:
            decays = decays_at(order_ref, chip)
            states = [advance(keys, order_ref, chip, h, decays, s) for h, s in enumerate(states)]
    for offset, out in enumerate((o0, o1, o2, o3)):
        out[...] = scr[sc_ref[1] ^ offset]


def enter_kernel(keys, sc_ref, first_ref, *refs):
    starts, (keep_ref, send_ref) = refs[:CHIPS], refs[CHIPS:]

    def fill(start_ref, after_ref):
        for offset in range(CHIPS):
            decays = decays_at(first_ref, offset)
            for h in range(2 * len(keys)):
                start = starts[offset][h]
                start_ref[offset, h] = start
                after_ref[offset, h] = advance(keys, first_ref, offset, h, decays, start)

    @pl.when(sc_ref[0] == 0)
    def _():
        fill(keep_ref, send_ref)

    @pl.when(sc_ref[0] == 1)
    def _():
        fill(send_ref, keep_ref)


def gates_kernel(gate_ref, gain_ref, out_ref):
    gates = gate_ref[...].astype(F32)
    gates = gates / (1.0 + jnp.exp(-gates))
    for h in range(VH):
        out_ref[:, head_slice(h)] = gates[:, head_slice(h)] * gain_ref[...]


def piece_columns(keys, own, sc_ref, offset):
    owner = sc_ref[0] if own else 1 - sc_ref[0]
    piece = owner * (VH // 2 // PIECE) + (sc_ref[1] ^ offset)
    start = (piece * PIECE + 2 * keys[0]) * DH
    return pl.ds(pl.multiple_of(start, 2 * DH), 2 * len(keys) * DH)


def finish_piece(keys, own, offset, sc_ref, gate_ref, state_ref, loc_ref, car_ref, out_ref):
    gates = gate_ref[:, piece_columns(keys, own, sc_ref, offset)]
    for h in range(2 * len(keys)):
        core = loc_ref[offset, h] + dot(car_ref[offset, h], state_ref[offset, h])
        mean_sq = jnp.mean(core * core, axis=1, keepdims=True)
        cols = head_slice(h)
        scaled = core * lax.rsqrt(mean_sq + 1e-06) * gates[:, cols]
        out_ref[offset, :, cols] = scaled.astype(BF16)


def finish_kernel(parts, sc_ref, gate_ref, *refs):
    for n, (keys, own) in enumerate(parts):
        for offset in range(CHIPS):
            ins = refs[3 * n : 3 * n + 3]
            finish_piece(keys, own, offset, sc_ref, gate_ref, *ins, refs[3 * len(parts) + n])


def finish(parts, place, gates, terms):
    return local_call(
        functools.partial(finish_kernel, parts),
        [place, gates, *sum(terms, [])],
        [jax.ShapeDtypeStruct((CHIPS, CH, 2 * len(keys) * DH), BF16) for keys, _ in parts],
        vmem_mib=4,
        name="finish",
    )


def last_kernel(earlier, keys, own, sc_ref, gate_ref, state_ref, loc_ref, car_ref, *refs):
    done_refs, (out_ref, scr, sems) = refs[: len(earlier)], refs[len(earlier) :]
    copies = []

    def send(source, cols):
        copies.append(pltpu.make_async_copy(source, out_ref.at[:, cols], sems.at[len(copies)]))
        copies[-1].start()

    for part, done_ref in zip(earlier, done_refs):
        for offset in range(CHIPS):
            send(done_ref.at[offset], piece_columns(*part, sc_ref, offset))
    for offset in range(CHIPS):
        finish_piece(keys, own, offset, sc_ref, gate_ref, state_ref, loc_ref, car_ref, scr)
        send(scr.at[offset], piece_columns(keys, own, sc_ref, offset))
    for copy in copies:
        copy.wait()


def finish_last(earlier, part, place, gates, done, terms):
    keys, own = part
    vmem = pl.BlockSpec(memory_space=pltpu.VMEM)
    args = [place, gates, *terms, *done]
    return pl.pallas_call(
        functools.partial(last_kernel, earlier, keys, own),
        out_shape=jax.ShapeDtypeStruct(gates.shape, BF16),
        in_specs=[pl.BlockSpec(memory_space=pltpu.SMEM)] + [vmem] * (len(args) - 1),
        out_specs=pl.BlockSpec(memory_space=pl.ANY),
        scratch_shapes=[
            pltpu.VMEM((CHIPS, CH, 2 * len(keys) * DH), BF16),
            pltpu.SemaphoreType.DMA((CHIPS * (len(earlier) + 1),)),
        ],
        cost_estimate=pl.CostEstimate(flops=100, bytes_accessed=100, transcendentals=0),
        compiler_params=pltpu.CompilerParams(vmem_limit_bytes=4 << 20),
        name="finish_last",
    )(*args)


def shift(block, distance):
    count = lax.axis_size("seq")
    return lax.ppermute(block, "seq", [(i, i + distance) for i in range(count - distance)])


def swap(block, distance):
    return lax.ppermute(block, "seq", [(i, i ^ distance) for i in range(lax.axis_size("seq"))])


def level_masks():
    t_at, s_at = np.arange(CH)[:, None], np.arange(CH)[None, :]
    return np.stack(
        [(t_at > s_at) & ((t_at ^ s_at) >> level == 1) for level in range(7)]
    ).astype(ml_dtypes.bfloat16)


def local(mixed_qkv, conv_weight, beta_logit, log_decay, gate_in, norm_gain):
    at = lax.axis_index("seq")
    last = at // (2 * CHIPS) == lax.axis_size("seq") // (2 * CHIPS) - 1
    place = jnp.stack([at % 2, (at // 2) % CHIPS, last.astype(at.dtype), (at < 2 * CHIPS).astype(at.dtype)])
    x, weight, last_rows = load(mixed_qkv, conv_weight)
    rim = shift(last_rows, 1)
    conv_out, rows = early_conv(place, x, weight, log_decay, beta_logit)
    shared = (x, rim, weight, conv_out, rows, jnp.asarray(level_masks()))
    chips = range(CHIPS)
    hop = swap if lax.axis_size("seq") == 4 * CHIPS else shift
    parts, terms, done = [], [], []
    (gates,) = local_call(
        gates_kernel,
        [gate_in, norm_gain[None]],
        [jax.ShapeDtypeStruct(gate_in.shape, F32)],
        scalars=0,
        vmem_mib=4,
        name="gates",
    )
    firsts, traveled, solved = [], [], []
    for keys in BANDS:
        theirs, mine = block_terms(keys, place, shared)
        other = swap(theirs[0], 1)
        first, sent = compose(keys, place, mine[0], other)
        firsts.append(first)
        traveled.append([swap(sent[n], 2 * n) if n else sent[0] for n in range(CHIPS)])
        solved += [*theirs[1:], *mine[1:]]
    all_queries = block_queries(place, shared, solved)
    turn, _ = lax.optimization_barrier((place, all_queries))

    for keys, first, pieces, queries in zip(BANDS, firsts, traveled, all_queries):
        count = 2 * len(keys)
        state_shape = jax.ShapeDtypeStruct((count, DH, DH), BF16)
        order_shape = jax.ShapeDtypeStruct((CHIPS, rows_of(keys), WIDE), BF16)
        entering = jnp.zeros((count, DH, DH), BF16)
        for _ in range(max(lax.axis_size("seq") // (2 * CHIPS) - 1, 1)):
            order, leaving = local_call(
                functools.partial(gather_kernel, keys),
                [turn, *pieces, entering],
                [order_shape, state_shape],
                name="gather",
            )
            entering = hop(leaving, 2 * CHIPS)
        spread = local_call(
            functools.partial(spread_kernel, keys),
            [place, order, entering],
            [state_shape] * CHIPS,
            [pltpu.VMEM((CHIPS, count, DH, DH), BF16)],
            name="spread",
        )
        starts = [swap(spread[n], 2 * n) if n else spread[0] for n in range(CHIPS)]
        states_shape = jax.ShapeDtypeStruct((CHIPS, count, DH, DH), BF16)
        keep, send = local_call(
            functools.partial(enter_kernel, keys),
            [turn if keys == BANDS[0] else lax.optimization_barrier((turn, gates))[0], first, *starts],
            [states_shape, states_shape],
            name="enter",
        )
        for own, state in ((1, keep), (0, swap(send, 1))):
            parts.append((keys, own))
            terms.append([state, *queries[own]])
    done = finish(parts[:-1], place, gates, terms[:-1])
    return finish_last(parts[:-1], parts[-1], place, gates, done, terms[-1])


def solution(mesh):
    spec = P(("groups", "seq"), None)
    return jax.shard_map(
        local,
        mesh=mesh,
        in_specs=(spec, P(), spec, spec, spec, P()),
        out_specs=spec,
        check_vma=False,
    )
```

```python
import functools

import jax
import jax.numpy as jnp
import ml_dtypes
import numpy as np
from jax import lax
from jax.experimental import pallas as pl
from jax.experimental.pallas import tpu as pltpu
from jax.sharding import PartitionSpec as P

KH = 16
VH = 32
DH = 128
CH = 128
CHIPS = 4
PIECE = 4
BANDS = ((0,), (1,))
WIDE = 2 * DH

F32 = jnp.float32
BF16 = jnp.bfloat16


def dot(a, b):
    return jnp.dot(a, b, preferred_element_type=F32)


def halves(x):
    high = x.astype(BF16)
    return high, (x - high.astype(F32)).astype(BF16)


def decay_rows(decays):
    decays = decays[:PIECE]
    high = decays.astype(BF16).astype(F32)
    return jnp.concatenate([high, decays - high], axis=0).astype(BF16)


def rows_of(keys):
    return 2 * len(keys) * DH + 2 * PIECE


def decays_of(rows):
    rows = rows.astype(F32)
    return rows[:PIECE] + rows[PIECE:]


def head_slice(h):
    return slice(h * DH, (h + 1) * DH)


def rows_kernel(decay_ref, logit_ref, rows_ref):
    s_at = lax.broadcasted_iota(jnp.int32, (CH, CH), 0)
    t_at = lax.broadcasted_iota(jnp.int32, (CH, CH), 1)
    cumulative = jnp.dot(
        decay_ref[...],
        (s_at <= t_at).astype(F32),
        precision=lax.Precision.HIGHEST,
        preferred_element_type=F32,
    )
    beta = 1.0 / (1.0 + jnp.exp(-logit_ref[...].astype(F32)))
    for g in range(VH // PIECE):
        rows_ref[g, :PIECE] = cumulative[g * PIECE : (g + 1) * PIECE]
        rows_ref[g, PIECE:] = beta[g * PIECE : (g + 1) * PIECE]


def taps(padded, w, height):
    total = padded(0) * w[0:1]
    for tap in range(1, 4):
        total = total + padded(tap) * w[tap : tap + 1]
    return (total / (1.0 + jnp.exp(-total))).astype(BF16)


def load_kernel(x_ref, w_ref, x_out, w_out, rim_out, sems):
    copies = [
        pltpu.make_async_copy(x_ref.at[CH - 4 :], rim_out, sems.at[0]),
        pltpu.make_async_copy(w_ref, w_out, sems.at[1]),
    ]
    step = CH // 4
    for i in range(4):
        part = pl.ds(i * step, step)
        copies.append(pltpu.make_async_copy(x_ref.at[part], x_out.at[part], sems.at[2 + i]))
    for copy in copies:
        copy.start()
    for copy in copies:
        copy.wait()


def load(mixed_qkv, conv_weight):
    vmem = pl.BlockSpec(memory_space=pltpu.VMEM)
    return pl.pallas_call(
        load_kernel,
        out_shape=[
            jax.ShapeDtypeStruct(mixed_qkv.shape, BF16),
            jax.ShapeDtypeStruct(conv_weight.shape, BF16),
            jax.ShapeDtypeStruct((4, mixed_qkv.shape[1]), BF16),
        ],
        in_specs=[pl.BlockSpec(memory_space=pl.ANY)] * 2,
        out_specs=[vmem] * 3,
        scratch_shapes=[pltpu.SemaphoreType.DMA((6,))],
        cost_estimate=pl.CostEstimate(flops=100, bytes_accessed=100, transcendentals=0),
        compiler_params=pltpu.CompilerParams(vmem_limit_bytes=4 << 20),
        name="load",
    )(*(pltpu.with_memory_space_constraint(a, pltpu.HBM) for a in (mixed_qkv, conv_weight)))


def conv_kernel(sc_ref, x_ref, w_ref, decay_ref, logit_ref, out_ref, rows_ref, scr):
    rows_kernel(decay_ref, logit_ref, rows_ref)
    owner = 1 - sc_ref[0]
    width = scr.shape[2]
    keys, values = KH // 2 * DH // width, VH // 2 * DH // width
    starts = [KH * DH + (owner * keys + i) * width for i in range(keys)]
    starts += [2 * KH * DH + (owner * values + i) * width for i in range(values)]
    for i, start in enumerate(starts):
        cols = pl.ds(pl.multiple_of(start, width), width)
        scr[i % 2] = x_ref[:, cols].astype(F32)
        w = w_ref[:, cols].astype(F32)
        out_ref[8:, cols] = taps(lambda tap: scr[i % 2, 5 + tap : 5 + tap + CH - 8, :], w, CH - 8)


def early_conv(place, x, conv_weight, log_decay, beta_logit):
    return local_call(
        conv_kernel,
        [place, x, conv_weight, log_decay.T, beta_logit.T],
        [
            jax.ShapeDtypeStruct(x.shape, BF16),
            jax.ShapeDtypeStruct((VH // PIECE, 2 * PIECE, CH), F32),
        ],
        [pltpu.VMEM((2, CH, 512), F32)],
        vmem_mib=4,
        name="conv",
    )


def convolved(x_ref, rim_ref, w_ref, scr, slot, column, width, conv_ref=None):
    cols = pl.ds(pl.multiple_of(column, DH), width)
    w = w_ref[:, cols].astype(F32)
    scr[slot, 4:8, :width] = rim_ref[:, cols].astype(F32)
    if conv_ref is None:
        scr[slot, 8 : 8 + CH, :width] = x_ref[:, cols].astype(F32)
        return taps(lambda tap: scr[slot, 5 + tap : 5 + tap + CH, :width], w, CH).astype(F32)
    scr[slot, 8:16, :width] = x_ref[:8, cols].astype(F32)
    first = taps(lambda tap: scr[slot, 5 + tap : 13 + tap, :width], w, 8)
    rest = conv_ref[:, cols].astype(F32)
    return jnp.concatenate([first.astype(F32), rest[8:]], axis=0)


def inverse_norms(rows, axis):
    return lax.rsqrt(jnp.sum(rows * rows, axis=axis, keepdims=True) + 1e-06)


def decay_pairs(rows, cols, h):
    return jnp.exp(jnp.minimum(cols[:, h : h + 1] - rows[h : h + 1], 0.0))


def token_order():
    t_at = lax.broadcasted_iota(jnp.int32, (CH, CH), 0)
    s_at = lax.broadcasted_iota(jnp.int32, (CH, CH), 1)
    return t_at, s_at


def terms_kernel(keys, sc_ref, x_ref, rim_ref, w_ref, conv_ref, rows_ref, masks_ref, *refs):
    theirs_refs, mine_refs, scr = refs[:3], refs[3:6], refs[6]
    t_at, s_at = token_order()
    strict = t_at > s_at
    unit = (t_at == s_at).astype(F32).astype(BF16)
    pieces = VH // 2 // PIECE
    kd, vd = len(keys) * DH, 2 * len(keys) * DH

    heads = []
    slot = 0
    for own, (ma_ref, solved_ref, key_ref) in enumerate((theirs_refs, mine_refs)):
        owner = sc_ref[0] if own else 1 - sc_ref[0]
        conv = functools.partial(
            convolved, x_ref, rim_ref, w_ref, scr, conv_ref=None if own else conv_ref
        )
        for offset in range(CHIPS):
            piece = owner * pieces + (sc_ref[1] ^ offset)
            key_at = piece * PIECE // 2 + keys[0]
            ck = conv(slot, (KH + key_at) * DH, kd)
            cv = conv(slot + 1, 2 * (KH + key_at) * DH, vd)
            slot += 2
            rows = rows_ref[piece]
            following = pltpu.roll(rows, CH - 1, axis=1)
            cols = rows.T
            grow_cols = jnp.exp(cols)
            tail_rows = jnp.exp(rows[:, CH - 1 : CH] - rows)
            ma_ref[offset, 2 * kd :, :] = decay_rows(
                jnp.broadcast_to(jnp.exp(rows[:, CH - 1 : CH]), (8, WIDE))
            )
            for g, key in enumerate(keys):
                k_f = ck[:, head_slice(g)]
                k_b = k_f.astype(BF16)
                key_ref[offset, g] = k_b
                k_t = k_f.T
                rk_col, rk_row = inverse_norms(k_f, 1), inverse_norms(k_t, 0)
                key_dot = dot(k_b, k_t.astype(BF16)) * rk_col * rk_row
                for i in range(2):
                    h = 2 * key + i
                    system = key_dot * decay_pairs(rows, cols, h)
                    system = jnp.where(strict, system, 0.0).astype(BF16)
                    beta_row = rows[4 + h : 5 + h]
                    gains = jnp.broadcast_to(beta_row * following[4 + h : 5 + h], (CH, CH)).astype(BF16)
                    high = jnp.broadcast_to(beta_row, (CH, CH)).astype(BF16)
                    heads.append(
                        dict(
                            out=(ma_ref, solved_ref, offset, 2 * g + i),
                            system=system,
                            inv=unit * high - system * masks_ref[0] * gains,
                            value=cv[:, head_slice(2 * g + i)].astype(BF16),
                            key=(k_f * (grow_cols[:, h : h + 1] * rk_col)).astype(BF16),
                            tail=(k_t * (rk_row * tail_rows[h : h + 1])).astype(BF16),
                        )
                    )

    for level in range(1, 7):
        mask = masks_ref[level]
        steps = [dot(p["inv"], p["system"] * mask).astype(BF16) for p in heads]
        steps = [dot(s, p["inv"]).astype(BF16) for s, p in zip(steps, heads)]
        for s, p in zip(steps, heads):
            p["inv"] = p["inv"] - s

    for p in heads:
        right = jnp.concatenate([p["key"], p["value"]], axis=1)
        p["solved"] = dot(
            p["inv"],
            right,
        ).astype(BF16)
    for p in heads:
        ma_ref, solved_ref, offset, h = p["out"]
        solved = p["solved"]
        solved_ref[offset, h] = solved
        ma_ref[offset, head_slice(h), :] = dot(p["tail"], solved).astype(BF16)


def local_call(
    kernel, args, out_shape, scratch=(), flops=100_000_000, vmem_mib=12, scalars=1, name=None
):
    vmem = pl.BlockSpec(memory_space=pltpu.VMEM)
    in_specs = [pl.BlockSpec(memory_space=pltpu.SMEM)] * scalars + [vmem] * (len(args) - scalars)
    return pl.pallas_call(
        kernel,
        out_shape=out_shape,
        in_specs=in_specs,
        out_specs=[vmem] * len(out_shape),
        scratch_shapes=list(scratch),
        cost_estimate=pl.CostEstimate(flops=100, bytes_accessed=100, transcendentals=0),
        compiler_params=pltpu.CompilerParams(vmem_limit_bytes=vmem_mib << 20),
        name=name,
    )(*args)


def block_terms(keys, place, shared):
    outs = [
        jax.ShapeDtypeStruct((CHIPS, rows_of(keys), WIDE), BF16),
        jax.ShapeDtypeStruct((CHIPS, 2 * len(keys), CH, WIDE), BF16),
        jax.ShapeDtypeStruct((CHIPS, len(keys), CH, DH), BF16),
    ] * 2
    out = local_call(
        functools.partial(terms_kernel, keys),
        [place, *shared],
        outs,
        [pltpu.VMEM((4 * CHIPS, CH + 8, 2 * len(keys) * DH), F32)],
        vmem_mib=40,
        name="terms",
    )
    return out[:3], out[3:]


def compose_kernel(keys, sc_ref, mine_ref, other_ref, first_ref, *sent_refs):
    count = 2 * len(keys)

    def join(first_in, second_in):
        for offset in range(CHIPS):
            first_g, second_g = decays_at(first_in, offset), decays_at(second_in, offset)
            first_ref[offset] = first_in[offset]
            sent_refs[offset][count * DH :, :] = decay_rows(first_g * second_g)
            for h in range(count):
                first, second = first_in[offset, head_slice(h)], second_in[offset, head_slice(h)]
                product = dot(second[:, :DH], first)
                at = 2 * keys[0] + h
                decay = first_g[at : at + 1, :DH]
                kept = jnp.concatenate(
                    [second[:, :DH].astype(F32) * decay, second[:, DH:].astype(F32)], axis=1
                )
                sent_refs[offset][head_slice(h), :] = (
                    first.astype(F32) * second_g[at : at + 1] - product + kept
                ).astype(BF16)

    @pl.when(sc_ref[0] == 0)
    def _():
        join(mine_ref, other_ref)

    @pl.when(sc_ref[0] == 1)
    def _():
        join(other_ref, mine_ref)


def compose(keys, place, mine, other):
    one = jax.ShapeDtypeStruct((rows_of(keys), WIDE), BF16)
    first, *sent = local_call(
        functools.partial(compose_kernel, keys),
        [place, mine, other],
        [jax.ShapeDtypeStruct(mine.shape, BF16)] + [one] * CHIPS,
        vmem_mib=16,
        name="compose",
    )
    return first, sent


def queries_kernel(sc_ref, x_ref, rim_ref, w_ref, rows_ref, *refs):
    count = len(BANDS)
    ins, outs, scr = refs[: 4 * count], refs[4 * count : 8 * count], refs[-1]
    t_at, s_at = token_order()
    heads = []
    for n in range(2 * count):
        keys, own = BANDS[n // 2], n % 2
        solved_ref, key_ref = ins[2 * n : 2 * n + 2]
        out = outs[2 * n : 2 * n + 2]
        owner = sc_ref[0] if own else 1 - sc_ref[0]
        for offset in range(CHIPS):
            piece = owner * (VH // 2 // PIECE) + (sc_ref[1] ^ offset)
            kd = len(keys) * DH
            key_at = piece * PIECE // 2 + keys[0]
            cq = convolved(x_ref, rim_ref, w_ref, scr, n * CHIPS + offset, key_at * DH, kd)
            rows = rows_ref[piece]
            cols = rows.T
            grow_cols = jnp.exp(cols)
            for g, key in enumerate(keys):
                q_f = cq[:, head_slice(g)]
                k_t = key_ref[offset, g].astype(F32).T
                rq_col = inverse_norms(q_f, 1) * DH ** (-0.5)
                query_dot = dot(q_f.astype(BF16), k_t.astype(BF16)) * rq_col * inverse_norms(k_t, 0)
                for i in range(2):
                    h = 2 * key + i
                    mixing = query_dot * decay_pairs(rows, cols, h)
                    mixing = halves(jnp.where(t_at >= s_at, mixing, 0.0))
                    query = q_f * (grow_cols[:, h : h + 1] * rq_col)
                    heads.append((solved_ref, out, offset, 2 * g + i, mixing, query))
    for solved_ref, (loc_ref, car_ref), offset, h, mixing, query in heads:
        solved = solved_ref[offset, h]
        both = dot(jnp.concatenate(mixing, axis=1), jnp.concatenate([solved, solved], axis=0))
        loc_ref[offset, h] = both[:, DH:]
        car_ref[offset, h] = (query - both[:, :DH]).astype(BF16)


def block_queries(place, shared, solved):
    outs = []
    for keys in BANDS:
        rows = (CHIPS, 2 * len(keys), CH, DH)
        outs += [jax.ShapeDtypeStruct(rows, F32), jax.ShapeDtypeStruct(rows, BF16)] * 2
    width = max(len(keys) for keys in BANDS) * DH
    out = local_call(
        queries_kernel,
        [place, *shared[:3], shared[4], *solved],
        outs,
        [pltpu.VMEM((2 * len(BANDS) * CHIPS, CH + 8, width), F32)],
        vmem_mib=28,
        name="queries",
    )
    return [(out[4 * b : 4 * b + 2], out[4 * b + 2 : 4 * b + 4]) for b in range(len(BANDS))]


def decays_at(ref, slot):
    return decays_of(ref[slot, ref.shape[1] - 2 * PIECE :])


def advance(keys, ref, slot, h, decays, state):
    mats = ref[slot, head_slice(h)]
    at = 2 * keys[0] + h
    moved = state.astype(F32) * decays[at : at + 1, :DH] - dot(mats[:, :DH], state)
    return (moved + mats[:, DH:].astype(F32)).astype(BF16)


def gather_kernel(keys, sc_ref, p0, p1, p2, p3, in_ref, order_ref, out_ref):
    for offset, piece in enumerate((p0, p1, p2, p3)):
        order_ref[sc_ref[1] ^ offset] = piece[...]

    @pl.when(sc_ref[2] == 0)
    def _():
        states = [in_ref[h] for h in range(2 * len(keys))]
        for chip in range(CHIPS):
            decays = decays_at(order_ref, chip)
            states = [advance(keys, order_ref, chip, h, decays, s) for h, s in enumerate(states)]
        for h, state in enumerate(states):
            out_ref[h] = state

    @pl.when(sc_ref[2] == 1)
    def _():
        out_ref[...] = jnp.zeros_like(out_ref)


def spread_kernel(keys, sc_ref, order_ref, in_ref, o0, o1, o2, o3, scr):
    keep = (1 - sc_ref[3]).astype(BF16)
    states = [in_ref[h] * keep for h in range(2 * len(keys))]
    for chip in range(CHIPS):
        for h, state in enumerate(states):
            scr[chip, h] = state
        if chip < CHIPS - 1:
            decays = decays_at(order_ref, chip)
            states = [advance(keys, order_ref, chip, h, decays, s) for h, s in enumerate(states)]
    for offset, out in enumerate((o0, o1, o2, o3)):
        out[...] = scr[sc_ref[1] ^ offset]


def enter_kernel(keys, sc_ref, first_ref, *refs):
    starts, (keep_ref, send_ref) = refs[:CHIPS], refs[CHIPS:]

    def fill(start_ref, after_ref):
        for offset in range(CHIPS):
            decays = decays_at(first_ref, offset)
            for h in range(2 * len(keys)):
                start = starts[offset][h]
                start_ref[offset, h] = start
                after_ref[offset, h] = advance(keys, first_ref, offset, h, decays, start)

    @pl.when(sc_ref[0] == 0)
    def _():
        fill(keep_ref, send_ref)

    @pl.when(sc_ref[0] == 1)
    def _():
        fill(send_ref, keep_ref)


def gates_kernel(gate_ref, gain_ref, out_ref):
    gates = gate_ref[...].astype(F32)
    gates = gates / (1.0 + jnp.exp(-gates))
    for h in range(VH):
        out_ref[:, head_slice(h)] = gates[:, head_slice(h)] * gain_ref[...]


def piece_columns(keys, own, sc_ref, offset):
    owner = sc_ref[0] if own else 1 - sc_ref[0]
    piece = owner * (VH // 2 // PIECE) + (sc_ref[1] ^ offset)
    start = (piece * PIECE + 2 * keys[0]) * DH
    return pl.ds(pl.multiple_of(start, 2 * DH), 2 * len(keys) * DH)


def finish_piece(keys, own, offset, sc_ref, gate_ref, state_ref, loc_ref, car_ref, out_ref):
    gates = gate_ref[:, piece_columns(keys, own, sc_ref, offset)]
    for h in range(2 * len(keys)):
        core = loc_ref[offset, h] + dot(car_ref[offset, h], state_ref[offset, h])
        mean_sq = jnp.mean(core * core, axis=1, keepdims=True)
        cols = head_slice(h)
        scaled = core * lax.rsqrt(mean_sq + 1e-06) * gates[:, cols]
        out_ref[offset, :, cols] = scaled.astype(BF16)


def finish_kernel(parts, sc_ref, gate_ref, *refs):
    for n, (keys, own) in enumerate(parts):
        for offset in range(CHIPS):
            ins = refs[3 * n : 3 * n + 3]
            finish_piece(keys, own, offset, sc_ref, gate_ref, *ins, refs[3 * len(parts) + n])


def finish(parts, place, gates, terms):
    return local_call(
        functools.partial(finish_kernel, parts),
        [place, gates, *sum(terms, [])],
        [jax.ShapeDtypeStruct((CHIPS, CH, 2 * len(keys) * DH), BF16) for keys, _ in parts],
        vmem_mib=4,
        name="finish",
    )


def last_kernel(earlier, keys, own, sc_ref, gate_ref, state_ref, loc_ref, car_ref, *refs):
    done_refs, (out_ref, scr, sems) = refs[: len(earlier)], refs[len(earlier) :]
    copies = []

    def send(source, cols):
        copies.append(pltpu.make_async_copy(source, out_ref.at[:, cols], sems.at[len(copies)]))
        copies[-1].start()

    for part, done_ref in zip(earlier, done_refs):
        for offset in range(CHIPS):
            send(done_ref.at[offset], piece_columns(*part, sc_ref, offset))
    for offset in range(CHIPS):
        finish_piece(keys, own, offset, sc_ref, gate_ref, state_ref, loc_ref, car_ref, scr)
        send(scr.at[offset], piece_columns(keys, own, sc_ref, offset))
    for copy in copies:
        copy.wait()


def finish_last(earlier, part, place, gates, done, terms):
    keys, own = part
    vmem = pl.BlockSpec(memory_space=pltpu.VMEM)
    args = [place, gates, *terms, *done]
    return pl.pallas_call(
        functools.partial(last_kernel, earlier, keys, own),
        out_shape=jax.ShapeDtypeStruct(gates.shape, BF16),
        in_specs=[pl.BlockSpec(memory_space=pltpu.SMEM)] + [vmem] * (len(args) - 1),
        out_specs=pl.BlockSpec(memory_space=pl.ANY),
        scratch_shapes=[
            pltpu.VMEM((CHIPS, CH, 2 * len(keys) * DH), BF16),
            pltpu.SemaphoreType.DMA((CHIPS * (len(earlier) + 1),)),
        ],
        cost_estimate=pl.CostEstimate(flops=100, bytes_accessed=100, transcendentals=0),
        compiler_params=pltpu.CompilerParams(vmem_limit_bytes=4 << 20),
        name="finish_last",
    )(*args)


def shift(block, distance):
    count = lax.axis_size("seq")
    return lax.ppermute(block, "seq", [(i, i + distance) for i in range(count - distance)])


def swap(block, distance):
    return lax.ppermute(block, "seq", [(i, i ^ distance) for i in range(lax.axis_size("seq"))])


def level_masks():
    t_at, s_at = np.arange(CH)[:, None], np.arange(CH)[None, :]
    return np.stack(
        [(t_at > s_at) & ((t_at ^ s_at) >> level == 1) for level in range(7)]
    ).astype(ml_dtypes.bfloat16)


def local(mixed_qkv, conv_weight, beta_logit, log_decay, gate_in, norm_gain):
    at = lax.axis_index("seq")
    last = at // (2 * CHIPS) == lax.axis_size("seq") // (2 * CHIPS) - 1
    place = jnp.stack([at % 2, (at // 2) % CHIPS, last.astype(at.dtype), (at < 2 * CHIPS).astype(at.dtype)])
    x, weight, last_rows = load(mixed_qkv, conv_weight)
    rim = shift(last_rows, 1)
    conv_out, rows = early_conv(place, x, weight, log_decay, beta_logit)
    shared = (x, rim, weight, conv_out, rows, jnp.asarray(level_masks()))
    chips = range(CHIPS)
    hop = swap if lax.axis_size("seq") == 4 * CHIPS else shift
    parts, terms, done = [], [], []
    (gates,) = local_call(
        gates_kernel,
        [gate_in, norm_gain[None]],
        [jax.ShapeDtypeStruct(gate_in.shape, F32)],
        scalars=0,
        vmem_mib=4,
        name="gates",
    )
    firsts, traveled, solved = [], [], []
    for keys in BANDS:
        theirs, mine = block_terms(keys, place, shared)
        other = swap(theirs[0], 1)
        first, sent = compose(keys, place, mine[0], other)
        firsts.append(first)
        traveled.append([swap(sent[n], 2 * n) if n else sent[0] for n in range(CHIPS)])
        solved += [*theirs[1:], *mine[1:]]
    all_queries = block_queries(place, shared, solved)
    turn, _ = lax.optimization_barrier((place, all_queries))

    for keys, first, pieces, queries in zip(BANDS, firsts, traveled, all_queries):
        count = 2 * len(keys)
        state_shape = jax.ShapeDtypeStruct((count, DH, DH), BF16)
        order_shape = jax.ShapeDtypeStruct((CHIPS, rows_of(keys), WIDE), BF16)
        entering = jnp.zeros((count, DH, DH), BF16)
        for _ in range(max(lax.axis_size("seq") // (2 * CHIPS) - 1, 1)):
            order, leaving = local_call(
                functools.partial(gather_kernel, keys),
                [place if keys == BANDS[0] else turn, *pieces, entering],
                [order_shape, state_shape],
                name="gather",
            )
            entering = hop(leaving, 2 * CHIPS)
        spread = local_call(
            functools.partial(spread_kernel, keys),
            [place, order, entering],
            [state_shape] * CHIPS,
            [pltpu.VMEM((CHIPS, count, DH, DH), BF16)],
            name="spread",
        )
        starts = [swap(spread[n], 2 * n) if n else spread[0] for n in range(CHIPS)]
        states_shape = jax.ShapeDtypeStruct((CHIPS, count, DH, DH), BF16)
        keep, send = local_call(
            functools.partial(enter_kernel, keys),
            [turn if keys == BANDS[0] else lax.optimization_barrier((turn, gates))[0], first, *starts],
            [states_shape, states_shape],
            name="enter",
        )
        for own, state in ((1, keep), (0, swap(send, 1))):
            parts.append((keys, own))
            terms.append([state, *queries[own]])
    done = finish(parts[:-1], place, gates, terms[:-1])
    return finish_last(parts[:-1], parts[-1], place, gates, done, terms[-1])


def solution(mesh):
    spec = P(("groups", "seq"), None)
    return jax.shard_map(
        local,
        mesh=mesh,
        in_specs=(spec, P(), spec, spec, spec, P()),
        out_specs=spec,
        check_vma=False,
    )
```
